32 devices in a mesh: req: 16 (over z, x, core), head: 2 (over y).
Axes of the slice: x: 2, y: 2, z: 4, core: 2. Of those that a mesh axis runs over, the one named last changes fastest.
Arguments:
- draft_ids: int32 [256, 16], P('req'), may hold values from 0 to 63999
- worker_slot: int32 [256], P('req'), may hold values from 0 to 255, as said below
- accepted: int32 [256], P('req'), may hold values from 0 to 16
- embedding: bfloat16 [64000, 2048], P('req', 'head'), may hold values from -120 to 120
- w_query: bfloat16 [2048, 2048], P('req', 'head'), may hold values from -0.125 to 0.125
- w_key: bfloat16 [2048, 2048], P('req', 'head'), may hold values from -0.125 to 0.125
- w_value: bfloat16 [2048, 4096], P('req', 'head'), may hold values from -0.125 to 0.125
- w_gate: bfloat16 [2048, 4096], P('req', 'head'), may hold values from -0.125 to 0.125
- old_state: bfloat16 [256, 8, 256, 512], P('req', 'head'), may hold values from -4 to 4
Outputs:
- hidden: bfloat16 [256, 16, 4096], P('req', None, 'head')
- new_state: bfloat16 [256, 8, 256, 512], P('req', 'head')
The draws below stay inside these ranges and needn't reach their ends.
Inputs may be any that keep to these rules, and one draw needn't show every extreme that they name: worker_slot is a permutation of 0 to 255; request r is handled by worker worker_slot[r] // 16 at position worker_slot[r] % 16; the 16 requests of one owner (aligned blocks of 16) go to 16 different workers.
All inputs are finite; a program needn't handle non-finite values.
Results may differ from the reference program's by a relative error of at most 0.0095.
Values may be sent and summed in bfloat16 or wider, within the bound.
No kernel may reach another device: no remote copies, remote signals or barrier semaphores. Data moves between devices by JAX's collectives and lax.ppermute only.
A program may use at most 192 MiB of HBM per device.

```python
import math
import jax
import jax.numpy as jnp
import numpy as np
from jax import lax

D = 2048
HEADS = 8
KD = 256
VD = 512
VOCAB = 64000
DRAFT = 16
REQ_DEV = 16
WORKERS = 16
REQUESTS = 256


def draw_worker_slot(key, part):
    key_shift, key_group, key_spot = jax.random.split(key, 3)
    shuffled = jax.random.permutation(key_shift, WORKERS).astype(jnp.int32)
    needed = (shuffled == 1) | (shuffled == WORKERS // 2) | (shuffled == WORKERS - 1)
    order = jnp.argsort(jnp.where(needed, 0, 1).astype(jnp.int32), stable=True)
    shifts = jnp.take(shuffled, order)[:REQ_DEV]
    group_of = jax.vmap(lambda inner: jax.random.permutation(inner, REQ_DEV))(jax.random.split(key_group, WORKERS))
    spot_of = jax.vmap(lambda inner: jax.random.permutation(inner, REQ_DEV))(jax.random.split(key_spot, WORKERS))
    owners = jnp.arange(WORKERS, dtype=jnp.int32)[:, None]
    workers = (owners + shifts[group_of]) % WORKERS
    position = spot_of[workers, group_of]
    return (workers * REQ_DEV + position).reshape(-1).astype(jnp.int32)


def draw_embedding(key, part):
    key_base, key_rows, key_cols = jax.random.split(key, 3)
    row_scale = jnp.exp(jax.random.uniform(key_rows, (VOCAB, 1), jnp.float32, 0.0, math.log(10.0)))
    col_scale = jnp.exp(jax.random.uniform(key_cols, (1, D), jnp.float32, 0.0, math.log(3.0)))
    base = jnp.clip(jax.random.normal(key_base, (VOCAB, D), jnp.float32), -4.0, 4.0)
    return (base * row_scale * col_scale).astype(jnp.bfloat16)


def draw_old_state(key, part):
    key_base, key_rows, key_cols = jax.random.split(key, 3)
    request_scale = jnp.exp(jax.random.uniform(key_rows, (REQUESTS, 1, 1, 1), jnp.float32, math.log(0.5), math.log(2.0)))
    column_scale = jnp.exp(jax.random.uniform(key_cols, (1, HEADS, 1, VD), jnp.float32, math.log(0.5), math.log(4.0)))
    base = jnp.clip(jax.random.normal(key_base, (REQUESTS, HEADS, KD, VD), jnp.float32), -4.0, 4.0)
    return (0.125 * base * request_scale * column_scale).astype(jnp.bfloat16)


def touch_ends(values, stream_key, least, top_value):
    longest = values.shape.index(max(values.shape))
    spots = []
    for shift in (0, 1):
        where = [jax.random.randint(jax.random.fold_in(stream_key, axis), (), 0, length) for axis, length in enumerate(values.shape)]
        where[longest] = (where[longest] + shift) % values.shape[longest]
        spots.append(tuple(where))
    return values.at[spots[0]].set(least).at[spots[1]].set(top_value)


def levels(key, dims, cuts, least, largest):
    gain = 1.0
    for dim, parts in cuts:
        draws = jax.random.uniform(jax.random.fold_in(jax.random.fold_in(key, 6), dim), (parts,), jnp.float32, least / len(cuts), largest / len(cuts))
        gain = gain * jnp.repeat(jnp.exp(draws), dims[dim] // parts).reshape((-1,) + (1,) * (len(dims) - 1 - dim))
    return gain


def rank_bounds(number_of, lean):
    portions = [(1 << 20) // math.isqrt(grade ** lean) + 1 for grade in range(1, number_of + 1)]
    deviation = 1 + sum(portions) // (1 << 30)
    return np.cumsum(np.array([max(1, weight // deviation) for weight in portions]))


def skewed_ids(own_key, dims, amount, skew):
    listing = rank_bounds(amount, skew)
    lot = jax.random.randint(jax.random.fold_in(own_key, 1), dims, 0, int(listing[amount - 1]))
    grade = jnp.searchsorted(jnp.asarray(listing, jnp.int32), lot, side="right")
    return jax.random.permutation(jax.random.fold_in(own_key, 2), amount)[grade].astype(jnp.int32)


def centred(own_key, shape, scale, bound, shards=(), held_as=jnp.bfloat16):
    drawn = scale * jax.random.normal(own_key, shape, jnp.float32)
    if shards:
        drawn = drawn * levels(own_key, shape, shards, -0.22, 0.18)
    return jnp.clip(drawn, -bound, bound).astype(held_as)


def setup_inputs(seed: int = 0) -> dict:
    key_of = jax.random.split(jax.random.key(seed), 10)
    return {
        "draft_ids": touch_ends(skewed_ids(key_of[0], (REQUESTS, DRAFT), VOCAB, 2), jax.random.fold_in(key_of[0], 3), 0, VOCAB - 1).astype(jnp.int32),
        "worker_slot": draw_worker_slot(jax.random.fold_in(key_of[9], 71), 0),
        "accepted": touch_ends(jax.random.randint(key_of[2], (REQUESTS,), 0, DRAFT + 1), jax.random.fold_in(key_of[2], 1), 0, DRAFT).astype(jnp.int32),
        "embedding": draw_embedding(jax.random.fold_in(key_of[9], 71), 0),
        "w_query": centred(key_of[4], (D, HEADS * KD), D ** -0.5, 0.125, ((0, 16), (1, 2))),
        "w_key": centred(key_of[5], (D, HEADS * KD), D ** -0.5, 0.125, ((0, 16), (1, 2))),
        "w_value": centred(key_of[6], (D, HEADS * VD), D ** -0.5, 0.125, ((0, 16), (1, 2))),
        "w_gate": centred(key_of[7], (D, HEADS * VD), D ** -0.5, 0.125, ((0, 16), (1, 2))),
        "old_state": draw_old_state(jax.random.fold_in(key_of[9], 71), 0),
    }


def layer_norm(values):
    center = lax.optimization_barrier(jnp.mean(values, axis=-1, keepdims=True))
    shifted = values - center
    spread = lax.optimization_barrier(jnp.mean(shifted * shifted, axis=-1, keepdims=True))
    return shifted * lax.rsqrt(spread + 1e-05)

def reference(draft_ids, worker_slot, accepted, embedding, w_query, w_key, w_value, w_gate, old_state):
    looked = jnp.take(embedding, draft_ids.reshape(-1), axis=0)
    normed = layer_norm(looked.astype(jnp.float32)).astype(jnp.bfloat16)
    queries = jnp.dot(normed, w_query, preferred_element_type=jnp.float32).astype(jnp.bfloat16)
    keys_scaled = (jnp.dot(normed, w_key, preferred_element_type=jnp.float32) * KD ** (-0.5)).astype(jnp.bfloat16)
    values_all = jnp.dot(normed, w_value, preferred_element_type=jnp.float32).astype(jnp.bfloat16)
    gates_all = jnp.dot(normed, w_gate, preferred_element_type=jnp.float32).astype(jnp.bfloat16)
    queries = queries.reshape(REQUESTS, DRAFT, HEADS, KD)
    keys_scaled = keys_scaled.reshape(REQUESTS, DRAFT, HEADS, KD)
    values_all = values_all.reshape(REQUESTS, DRAFT, HEADS, VD)
    gates_all = gates_all.reshape(REQUESTS, DRAFT, HEADS, VD)
    positions = jnp.arange(DRAFT, dtype=jnp.float32)
    distance = positions[:, None] - positions[None, :]
    causal = distance >= 0.0
    counts = accepted.astype(jnp.float32)[:, None]
    remaining = jnp.maximum(counts - 1.0 - positions[None, :], 0.0)
    within = positions[None, :] < counts
    decay_rate = 1.0 - jnp.exp2(-5.0 - jnp.arange(HEADS, dtype=jnp.float32))
    outputs = []
    states = []
    for head_index in range(HEADS):
        head_rate = decay_rate[head_index]
        query_head = queries[:, :, head_index].astype(jnp.float32)
        key_head = keys_scaled[:, :, head_index].astype(jnp.float32)
        value_head = values_all[:, :, head_index].astype(jnp.float32)
        gate_head = gates_all[:, :, head_index].astype(jnp.float32)
        start_state = old_state[:, head_index].astype(jnp.float32)
        decay_mask = jnp.where(causal, jnp.power(head_rate, jnp.maximum(distance, 0.0)), 0.0)
        scores = jnp.einsum('rtk,rsk->rts', query_head, key_head) * decay_mask[None]
        weights = lax.optimization_barrier(scores.astype(jnp.bfloat16)).astype(jnp.float32)
        inside_terms = jnp.einsum('rts,rsv->rtv', weights, value_head)
        state_terms = jnp.einsum('rtk,rkv->rtv', query_head, start_state) * jnp.power(head_rate, positions + 1.0)[None, :, None]
        mixture = layer_norm(inside_terms + state_terms)
        outputs.append((jax.nn.silu(gate_head) * mixture).astype(jnp.bfloat16))
        scale_rows = jnp.where(within, jnp.power(head_rate, remaining), 0.0)
        kept_keys = lax.optimization_barrier((key_head * scale_rows[:, :, None]).astype(jnp.bfloat16)).astype(jnp.float32)
        updated = jnp.einsum('rsk,rsv->rkv', kept_keys, value_head) + jnp.power(head_rate, counts)[:, :, None] * start_state
        states.append(updated.astype(jnp.bfloat16))
    hidden = jnp.stack(outputs, axis=2).reshape(REQUESTS, DRAFT, HEADS * VD)
    placed = jnp.zeros_like(hidden).at[worker_slot].set(hidden)
    return (placed, jnp.stack(states, axis=1))
```

```python
import jax
import jax.numpy as jnp
from jax import lax
from jax.experimental import pallas as pl
from jax.experimental.pallas import tpu as pltpu
from jax.sharding import PartitionSpec as P

ZLEN = 4


def layer_norm(values):
    center = jnp.mean(values, axis=-1, keepdims=True)
    shifted = values - center
    spread = jnp.mean(shifted * shifted, axis=-1, keepdims=True)
    return shifted * lax.rsqrt(spread + 1e-05)


def retention(queries, keys_scaled, values_all, gates_all, start_state, counts_int, head_ids):
    row_count = queries.shape[0]
    draft_len = queries.shape[1]
    heads_dev = start_state.shape[1]
    key_dim = start_state.shape[2]
    value_dim = start_state.shape[3]
    query_heads = queries.reshape(row_count, draft_len, heads_dev, key_dim)
    key_heads = keys_scaled.reshape(row_count, draft_len, heads_dev, key_dim)
    value_heads = values_all.reshape(row_count, draft_len, heads_dev, value_dim)
    gate_heads = gates_all.reshape(row_count, draft_len, heads_dev, value_dim)
    decay_rate = 1.0 - jnp.exp2(-5.0 - head_ids)
    positions = jnp.arange(draft_len, dtype=jnp.float32)
    distance = positions[:, None] - positions[None, :]
    causal = distance >= 0.0
    decay_mask = jnp.where(
        causal[None], jnp.power(decay_rate[:, None, None], jnp.maximum(distance, 0.0)[None]), 0.0
    )
    scores = (
        jnp.einsum("nthk,nshk->nhts", query_heads, key_heads, preferred_element_type=jnp.float32)
        * decay_mask[None]
    )
    weights = scores.astype(jnp.bfloat16)
    inside_terms = jnp.einsum(
        "nhts,nshv->nthv", weights, value_heads, preferred_element_type=jnp.float32
    )
    state_terms = jnp.einsum(
        "nthk,nhkv->nthv", query_heads, start_state, preferred_element_type=jnp.float32
    )
    state_terms = (
        state_terms * jnp.power(decay_rate[None, :], positions[:, None] + 1.0)[None, :, :, None]
    )
    mixture = layer_norm(inside_terms + state_terms)
    hidden = (jax.nn.silu(gate_heads.astype(jnp.float32)) * mixture).astype(jnp.bfloat16)
    hidden = hidden.reshape(row_count, draft_len, heads_dev * value_dim)
    counts = counts_int.astype(jnp.float32)[:, None]
    remaining = jnp.maximum(counts - 1.0 - positions[None, :], 0.0)
    within = positions[None, :] < counts
    scale_rows = jnp.where(
        within[:, :, None], jnp.power(decay_rate[None, None, :], remaining[:, :, None]), 0.0
    )
    kept_keys = (key_heads.astype(jnp.float32) * scale_rows[..., None]).astype(jnp.bfloat16)
    updated = jnp.einsum(
        "nshk,nshv->nhkv", kept_keys, value_heads, preferred_element_type=jnp.float32
    )
    updated = updated + jnp.power(decay_rate[None, :], counts)[
        :, :, None, None
    ] * start_state.astype(jnp.float32)
    return (hidden, updated.astype(jnp.bfloat16))


def token_rows(draft_ids, worker_slot, embedding):
    width = lax.axis_size("req")
    own_rows, draft_len = draft_ids.shape
    count = own_rows * draft_len
    vocab_rows, cols = embedding.shape
    cap = -(-2 * count // width)
    lanes = -(-(cap + 2) // 128) * 128
    ids = draft_ids.reshape(count)
    holder = ids // vocab_rows
    local = ids - holder * vocab_rows
    order = jnp.arange(count, dtype=jnp.int32)
    same = ids[:, None] == ids[None, :]
    first_at = jnp.min(jnp.where(same, order[None, :], count), axis=1)
    is_first = first_at == order
    peers = is_first[None, :] & (holder[:, None] == holder[None, :])
    rank = jnp.sum((peers & (order[None, :] < first_at[:, None])).astype(jnp.int32), axis=1)
    most = jnp.max(jnp.sum(peers.astype(jnp.int32), axis=1))
    own_rounds = (most + cap - 1) // cap

    def requests(turn):
        spot = jnp.where(is_first & (rank // cap == turn), holder * cap + rank % cap, -1)
        hit = spot[None, :] == jnp.arange(width * cap, dtype=jnp.int32)[:, None]
        return jnp.sum(jnp.where(hit, local[None, :], 0), axis=1).reshape(width, cap)

    def rows_for(wanted):
        picked = jnp.take(embedding, wanted.reshape(width * cap), axis=0, mode="clip")
        got = lax.all_to_all(
            picked.reshape(width, cap, cols), "req", split_axis=0, concat_axis=0, tiled=True
        )
        return jnp.take(got.reshape(width * cap, cols), holder * cap + rank % cap, axis=0, mode="clip")

    target = worker_slot // own_rows
    place = worker_slot - target * own_rows
    to_target = target[None, :] == jnp.arange(width, dtype=jnp.int32)[:, None]
    place_for = jnp.sum(jnp.where(to_target, place[None, :], 0), axis=1)
    table = jnp.concatenate(
        [
            requests(0),
            place_for[:, None],
            jnp.full((width, 1), own_rounds, jnp.int32),
            jnp.zeros((width, lanes - cap - 2), jnp.int32),
        ],
        axis=1,
    )
    heard = lax.all_to_all(table, "req", split_axis=0, concat_axis=0, tiled=True)
    place_of = heard[:, cap]
    rounds = jnp.max(heard[:, cap + 1])
    tokens = rows_for(heard[:, :cap])

    def more(carry):
        return carry[0] < rounds

    def step(carry):
        turn, held = carry
        wanted = lax.all_to_all(
            requests(turn), "req", split_axis=0, concat_axis=0, tiled=True
        )
        fresh = rows_for(wanted)
        return turn + 1, jnp.where((rank // cap == turn)[:, None], fresh, held)

    _, tokens = lax.while_loop(more, step, (jnp.int32(1), tokens))
    return tokens, place_of


def project_kernel(zpos_ref, normed_ref, *refs):
    pieces, out_ref = refs[:-1], refs[-1]
    depth = pieces[0].shape[0]
    total = None
    for step, piece in enumerate(pieces):
        shard = lax.rem(zpos_ref[0] + (len(pieces) - step), len(pieces))
        start = pl.multiple_of(shard * depth, 128)
        term = jnp.dot(
            normed_ref[:, pl.ds(start, depth)], piece[...], preferred_element_type=jnp.float32
        )
        total = term if total is None else total + term
    out_ref[...] = total.astype(out_ref.dtype)


def project(zpos, normed, pieces):
    rows, width = normed.shape[0], pieces[0].shape[1]
    block = 256
    depth = pieces[0].shape[0]
    return pl.pallas_call(
        project_kernel,
        out_shape=jax.ShapeDtypeStruct((rows, width), jnp.bfloat16),
        grid_spec=pltpu.PrefetchScalarGridSpec(
            num_scalar_prefetch=1,
            grid=(rows // block,),
            in_specs=[pl.BlockSpec((block, normed.shape[1]), lambda i, z: (i, 0))]
            + [pl.BlockSpec((depth, width), lambda i, z: (0, 0)) for _ in pieces],
            out_specs=pl.BlockSpec((block, width), lambda i, z: (i, 0)),
        ),
        cost_estimate=pl.CostEstimate(
            flops=2 * rows * width * normed.shape[1],
            bytes_accessed=2 * (rows * normed.shape[1] + normed.shape[1] * width + rows * width),
            transcendentals=0,
        ),
        name="project",
    )(zpos, normed, *pieces)


GROUP = 4


def hidden_kernel(head, key_dim, value_dim, to_ref, rate_ref, mix_ref, state_ref, out_ref):
    draft = mix_ref.shape[1]
    log_rate = rate_ref[head]
    t_pos = lax.broadcasted_iota(jnp.int32, (draft, draft), 0)
    s_pos = lax.broadcasted_iota(jnp.int32, (draft, draft), 1)
    away = (t_pos - s_pos).astype(jnp.float32)
    mask = jnp.where(away >= 0.0, jnp.exp(jnp.maximum(away, 0.0) * log_rate), 0.0)
    after = lax.broadcasted_iota(jnp.int32, (draft, value_dim), 0).astype(jnp.float32) + 1.0
    fade = jnp.exp(after * log_rate)
    base = pl.program_id(0) * GROUP
    for r in range(GROUP):
        query = mix_ref[r, :, :key_dim]
        keys = mix_ref[r, :, key_dim : 2 * key_dim] * jnp.bfloat16(key_dim**-0.5)
        values = mix_ref[r, :, 2 * key_dim : 2 * key_dim + value_dim]
        gate = mix_ref[r, :, 2 * key_dim + value_dim :].astype(jnp.float32)
        scores = lax.dot_general(
            query, keys, (((1,), (1,)), ((), ())), preferred_element_type=jnp.float32
        )
        weights = (scores * mask).astype(jnp.bfloat16)
        inside = jnp.dot(weights, values, preferred_element_type=jnp.float32)
        carried = jnp.dot(query, state_ref[r, 0], preferred_element_type=jnp.float32)
        mixture = layer_norm(inside + carried * fade)
        out_ref[to_ref[base + r]] = (jax.nn.silu(gate) * mixture).astype(jnp.bfloat16)


def hidden_of(head, target, log_rate, mix, state):
    rows, draft, width = mix.shape
    _, _, key_dim, value_dim = state.shape
    return pl.pallas_call(
        lambda *refs: hidden_kernel(head, key_dim, value_dim, *refs),
        out_shape=jax.ShapeDtypeStruct((rows, draft, value_dim), jnp.bfloat16),
        grid_spec=pltpu.PrefetchScalarGridSpec(
            num_scalar_prefetch=2,
            grid=(rows // GROUP,),
            in_specs=[
                pl.BlockSpec((GROUP, draft, width), lambda i, *_: (i, 0, 0)),
                pl.BlockSpec((GROUP, 1, key_dim, value_dim), lambda i, *_: (i, head, 0, 0)),
            ],
            out_specs=pl.BlockSpec((rows, draft, value_dim), lambda i, *_: (0, 0, 0)),
        ),
        cost_estimate=pl.CostEstimate(
            flops=2 * rows * draft * key_dim * value_dim * 8,
            bytes_accessed=2 * rows * (key_dim * value_dim + draft * (width + value_dim)),
            transcendentals=rows * draft * value_dim,
        ),
        name="hidden",
    )(target, log_rate, mix, state)


def update_kernel(head, key_dim, value_dim, held, acc_ref, rate_ref, mix_ref, state_ref, *refs):
    out_ref = refs[-1]
    draft = mix_ref.shape[1]
    log_rate = rate_ref[head]
    spot = lax.broadcasted_iota(jnp.int32, (draft, key_dim), 0)
    base = pl.program_id(0) * GROUP
    for r in range(GROUP):
        taken = acc_ref[base + r]
        left = jnp.maximum(taken - 1 - spot, 0).astype(jnp.float32)
        scale = jnp.where(spot < taken, jnp.exp(left * log_rate), 0.0)
        keys = (mix_ref[r, :, key_dim : 2 * key_dim] * jnp.bfloat16(key_dim**-0.5)).astype(
            jnp.float32
        )
        kept = (keys * scale).astype(jnp.bfloat16)
        values = mix_ref[r, :, 2 * key_dim : 2 * key_dim + value_dim]
        fresh = lax.dot_general(
            kept, values, (((0,), (0,)), ((), ())), preferred_element_type=jnp.float32
        )
        fade = jnp.exp(
            jnp.full((key_dim, value_dim), taken.astype(jnp.float32) * log_rate, jnp.float32)[:8]
        )[:1]
        out_ref[r, 0] = (fresh + fade * state_ref[r, 0].astype(jnp.float32)).astype(jnp.bfloat16)


def update_of(head, accepted, log_rate, mix, state, earlier):
    rows, draft, width = mix.shape
    _, _, key_dim, value_dim = state.shape
    spec = pl.BlockSpec((GROUP, 1, key_dim, value_dim), lambda i, *_: (i, head, 0, 0))
    more = () if earlier is None else (earlier,)
    return pl.pallas_call(
        lambda *refs: update_kernel(head, key_dim, value_dim, bool(more), *refs),
        out_shape=jax.ShapeDtypeStruct(state.shape, jnp.bfloat16),
        grid_spec=pltpu.PrefetchScalarGridSpec(
            num_scalar_prefetch=2,
            grid=(rows // GROUP,),
            in_specs=[pl.BlockSpec((GROUP, draft, width), lambda i, *_: (i, 0, 0)), spec]
            + [pl.BlockSpec(memory_space=pl.ANY) for _ in more],
            out_specs=spec,
        ),
        input_output_aliases={4: 0} if more else {},
        cost_estimate=pl.CostEstimate(
            flops=2 * rows * draft * key_dim * value_dim * 8,
            bytes_accessed=4 * rows * key_dim * value_dim,
            transcendentals=0,
        ),
        name="update",
    )(accepted, log_rate, mix, state, *more)


def settle_kernel(place_ref, *refs):
    parts, out_ref = refs[:-1], refs[-1]
    value_dim = parts[0].shape[2]
    for s in range(parts[0].shape[0]):
        row = place_ref[s]
        for j, part in enumerate(parts):
            out_ref[row, :, j * value_dim : (j + 1) * value_dim] = part[s]


def settle(place_of, parts):
    rows, draft, value_dim = parts[0].shape
    whole = (rows, draft, value_dim * len(parts))
    return pl.pallas_call(
        settle_kernel,
        out_shape=jax.ShapeDtypeStruct(whole, jnp.bfloat16),
        grid_spec=pltpu.PrefetchScalarGridSpec(
            num_scalar_prefetch=1,
            grid=(1,),
            in_specs=[
                pl.BlockSpec(part.shape, lambda i, *_: (0, 0, 0)) for part in parts
            ],
            out_specs=pl.BlockSpec(whole, lambda i, *_: (0, 0, 0)),
        ),
        name="settle",
    )(place_of, *parts)


def canonical(member, pieces):
    pieces = list(pieces)
    bit = 1
    while bit < len(pieces):
        swap = (member & bit) != 0
        pieces = [jnp.where(swap, pieces[k ^ bit], pieces[k]) for k in range(len(pieces))]
        bit *= 2
    return pieces


def swap_perm(group, k):
    return [(z * group + m, z * group + (m ^ k)) for z in range(ZLEN) for m in range(group)]


def ring_perm(group, shift):
    return [
        (z * group + m, ((z + shift) % ZLEN) * group + m) for z in range(ZLEN) for m in range(group)
    ]


def fast_device(
    draft_ids, worker_slot, accepted, embedding, w_query, w_key, w_value, w_gate, old_state
):
    own_rows, draft = draft_ids.shape
    heads = old_state.shape[1]
    key_dim, value_dim = old_state.shape[2:]
    group = lax.axis_size("req") // ZLEN
    member = lax.axis_index("req") % group
    zpos = lax.axis_index("req") // group
    count = own_rows * draft
    share = 2 * (key_dim + value_dim) // group

    gathered = []
    for j in range(heads):
        whole = jnp.concatenate(
            [
                w_query[:, j * key_dim : (j + 1) * key_dim],
                w_key[:, j * key_dim : (j + 1) * key_dim],
                w_value[:, j * value_dim : (j + 1) * value_dim],
                w_gate[:, j * value_dim : (j + 1) * value_dim],
            ],
            axis=1,
        )
        parts = []
        for k in range(group):
            part = lax.dynamic_slice_in_dim(whole, (member ^ k) * share, share, axis=1)
            parts.append(part if k == 0 else lax.ppermute(part, "req", swap_perm(group, k)))
        plane = jnp.concatenate(canonical(member, parts), axis=0)
        one = lax.ppermute(plane, "req", ring_perm(group, 1))
        three = lax.ppermute(plane, "req", ring_perm(group, 3))
        two = lax.ppermute(one, "req", ring_perm(group, 1))
        gathered.append((plane, one, two, three))

    half, place_of = token_rows(draft_ids, worker_slot, embedding)
    other = lax.ppermute(half, "head", [(0, 1), (1, 0)])
    low = lax.axis_index("head") == 0
    tokens = jnp.concatenate([jnp.where(low, half, other), jnp.where(low, other, half)], axis=1)
    normed = layer_norm(tokens.astype(jnp.float32)).astype(jnp.bfloat16)
    bit = 1
    while bit < group:
        there = lax.ppermute(normed, "req", swap_perm(group, bit))
        swap = (member & bit) != 0
        normed = jnp.concatenate(
            [jnp.where(swap, there, normed), jnp.where(swap, normed, there)], axis=0
        )
        bit *= 2

    head_ids = (lax.axis_index("head") * heads + jnp.arange(heads, dtype=jnp.int32)).astype(
        jnp.float32
    )
    log_rate = jnp.log1p(-jnp.exp2(-5.0 - head_ids))
    target = worker_slot // own_rows
    parts_out, new_state = [], None
    for j in range(heads):
        result = project(zpos.reshape(1).astype(jnp.int32), normed, gathered[j])
        parts = []
        for k in range(group):
            part = lax.dynamic_slice_in_dim(result, (member ^ k) * count, count, axis=0)
            parts.append(part if k == 0 else lax.ppermute(part, "req", swap_perm(group, k)))
        mix = jnp.concatenate(canonical(member, parts), axis=1).reshape(own_rows, draft, -1)
        answer = hidden_of(j, target, log_rate, mix, old_state)
        parts_out.append(
            lax.all_to_all(answer, "req", split_axis=0, concat_axis=0, tiled=True)
        )
        new_state = update_of(j, accepted, log_rate, mix, old_state, new_state)
    return settle(place_of, parts_out), new_state


def plain_device(
    draft_ids, worker_slot, accepted, embedding, w_query, w_key, w_value, w_gate, old_state
):
    own_rows, draft = draft_ids.shape
    tables = [
        lax.all_gather(table, "req", axis=0, tiled=True)
        for table in (w_query, w_key, w_value, w_gate)
    ]
    half, place_of = token_rows(draft_ids, worker_slot, embedding)
    tokens = lax.all_gather(half, "head", axis=1, tiled=True)
    normed = layer_norm(tokens.astype(jnp.float32)).astype(jnp.bfloat16)
    raw = [jnp.dot(normed, table, preferred_element_type=jnp.float32) for table in tables]
    raw[1] = raw[1] * old_state.shape[2] ** (-0.5)
    made = [one.astype(jnp.bfloat16).reshape(own_rows, draft, -1) for one in raw]
    heads = old_state.shape[1]
    head_ids = (lax.axis_index("head") * heads + jnp.arange(heads, dtype=jnp.int32)).astype(
        jnp.float32
    )
    answer, new_state = retention(*made, old_state, accepted, head_ids)
    width = lax.axis_size("req")
    target = worker_slot // own_rows
    ahead = jnp.zeros((width,) + answer.shape[1:], answer.dtype).at[target].set(answer)
    received = lax.all_to_all(ahead, "req", split_axis=0, concat_axis=0, tiled=True)
    mine = lax.axis_index("req")
    valid = lax.all_to_all(
        (target[None, :] == jnp.arange(width)[:, None]).any(axis=1).astype(jnp.int32)[:, None],
        "req", split_axis=0, concat_axis=0, tiled=True,
    )[:, 0]
    spot = jnp.where(valid > 0, place_of, own_rows)
    hidden = jnp.zeros_like(answer).at[spot].set(received, mode="drop")
    return hidden, new_state


def solution(mesh):
    width, head_width = mesh.shape["req"], mesh.shape["head"]
    fast = head_width == 2 and width == 16
    return jax.shard_map(
        fast_device if fast else plain_device,
        mesh=mesh,
        in_specs=(
            P("req", None),
            P("req"),
            P("req"),
            P("req", "head"),
            P("req", "head"),
            P("req", "head"),
            P("req", "head"),
            P("req", "head"),
            P("req", "head", None, None),
        ),
        out_specs=(P("req", None, "head"), P("req", "head", None, None)),
        check_vma=False,
    )
```

```python
import jax
import jax.numpy as jnp
from jax import lax
from jax.experimental import pallas as pl
from jax.experimental.pallas import tpu as pltpu
from jax.sharding import PartitionSpec as P

ZLEN = 4


def layer_norm(values):
    center = jnp.mean(values, axis=-1, keepdims=True)
    shifted = values - center
    spread = jnp.mean(shifted * shifted, axis=-1, keepdims=True)
    return shifted * lax.rsqrt(spread + 1e-05)


def retention(queries, keys_scaled, values_all, gates_all, start_state, counts_int, head_ids):
    row_count = queries.shape[0]
    draft_len = queries.shape[1]
    heads_dev = start_state.shape[1]
    key_dim = start_state.shape[2]
    value_dim = start_state.shape[3]
    query_heads = queries.reshape(row_count, draft_len, heads_dev, key_dim)
    key_heads = keys_scaled.reshape(row_count, draft_len, heads_dev, key_dim)
    value_heads = values_all.reshape(row_count, draft_len, heads_dev, value_dim)
    gate_heads = gates_all.reshape(row_count, draft_len, heads_dev, value_dim)
    decay_rate = 1.0 - jnp.exp2(-5.0 - head_ids)
    positions = jnp.arange(draft_len, dtype=jnp.float32)
    distance = positions[:, None] - positions[None, :]
    causal = distance >= 0.0
    decay_mask = jnp.where(
        causal[None], jnp.power(decay_rate[:, None, None], jnp.maximum(distance, 0.0)[None]), 0.0
    )
    scores = (
        jnp.einsum("nthk,nshk->nhts", query_heads, key_heads, preferred_element_type=jnp.float32)
        * decay_mask[None]
    )
    weights = scores.astype(jnp.bfloat16)
    inside_terms = jnp.einsum(
        "nhts,nshv->nthv", weights, value_heads, preferred_element_type=jnp.float32
    )
    state_terms = jnp.einsum(
        "nthk,nhkv->nthv", query_heads, start_state, preferred_element_type=jnp.float32
    )
    state_terms = (
        state_terms * jnp.power(decay_rate[None, :], positions[:, None] + 1.0)[None, :, :, None]
    )
    mixture = layer_norm(inside_terms + state_terms)
    hidden = (jax.nn.silu(gate_heads.astype(jnp.float32)) * mixture).astype(jnp.bfloat16)
    hidden = hidden.reshape(row_count, draft_len, heads_dev * value_dim)
    counts = counts_int.astype(jnp.float32)[:, None]
    remaining = jnp.maximum(counts - 1.0 - positions[None, :], 0.0)
    within = positions[None, :] < counts
    scale_rows = jnp.where(
        within[:, :, None], jnp.power(decay_rate[None, None, :], remaining[:, :, None]), 0.0
    )
    kept_keys = (key_heads.astype(jnp.float32) * scale_rows[..., None]).astype(jnp.bfloat16)
    updated = jnp.einsum(
        "nshk,nshv->nhkv", kept_keys, value_heads, preferred_element_type=jnp.float32
    )
    updated = updated + jnp.power(decay_rate[None, :], counts)[
        :, :, None, None
    ] * start_state.astype(jnp.float32)
    return (hidden, updated.astype(jnp.bfloat16))


def after(value, *needed):
    return lax.optimization_barrier((value, needed))[0]


def token_rows(draft_ids, worker_slot, embedding, asked=None, found=None):
    width = lax.axis_size("req")
    own_rows, draft_len = draft_ids.shape
    count = own_rows * draft_len
    vocab_rows, cols = embedding.shape
    cap = -(-2 * count // width)
    lanes = -(-(cap + 2) // 128) * 128
    ids = draft_ids.reshape(count)
    holder = ids // vocab_rows
    local = ids - holder * vocab_rows
    order = jnp.arange(count, dtype=jnp.int32)
    same = ids[:, None] == ids[None, :]
    first_at = jnp.min(jnp.where(same, order[None, :], count), axis=1)
    is_first = first_at == order
    peers = is_first[None, :] & (holder[:, None] == holder[None, :])
    rank = jnp.sum((peers & (order[None, :] < first_at[:, None])).astype(jnp.int32), axis=1)
    most = jnp.max(jnp.sum(peers.astype(jnp.int32), axis=1))
    own_rounds = (most + cap - 1) // cap

    def requests(turn):
        spot = jnp.where(is_first & (rank // cap == turn), holder * cap + rank % cap, -1)
        hit = spot[None, :] == jnp.arange(width * cap, dtype=jnp.int32)[:, None]
        return jnp.sum(jnp.where(hit, local[None, :], 0), axis=1).reshape(width, cap)

    def rows_for(wanted, needed=None):
        picked = jnp.take(embedding, wanted.reshape(width * cap), axis=0, mode="clip")
        if needed is not None:
            picked = after(picked, needed)
        got = lax.all_to_all(
            picked.reshape(width, cap, cols), "req", split_axis=0, concat_axis=0, tiled=True
        )
        return jnp.take(got.reshape(width * cap, cols), holder * cap + rank % cap, axis=0, mode="clip")

    target = worker_slot // own_rows
    place = worker_slot - target * own_rows
    to_target = target[None, :] == jnp.arange(width, dtype=jnp.int32)[:, None]
    place_for = jnp.sum(jnp.where(to_target, place[None, :], 0), axis=1)
    table = jnp.concatenate(
        [
            requests(0),
            place_for[:, None],
            jnp.full((width, 1), own_rounds, jnp.int32),
            jnp.zeros((width, lanes - cap - 2), jnp.int32),
        ],
        axis=1,
    )
    heard = lax.all_to_all(table, "req", split_axis=0, concat_axis=0, tiled=True)
    if asked is not None:
        heard = after(heard, asked)
    place_of = heard[:, cap]
    rounds = jnp.max(heard[:, cap + 1])
    tokens = rows_for(heard[:, :cap], found)

    def more(carry):
        return carry[0] < rounds

    def step(carry):
        turn, held = carry
        wanted = lax.all_to_all(
            requests(turn), "req", split_axis=0, concat_axis=0, tiled=True
        )
        fresh = rows_for(wanted)
        return turn + 1, jnp.where((rank // cap == turn)[:, None], fresh, held)

    def finish(first):
        return lax.while_loop(more, step, (jnp.int32(1), first))[1]

    return tokens, finish, place_of


def pack_kernel(heads, chunks, group, member_ref, q_ref, k_ref, v_ref, g_ref, *refs):
    outs, whole = refs[:-1], refs[-1]
    key_dim, value_dim = q_ref.shape[1] // heads, v_ref.shape[1] // heads
    share = 2 * (key_dim + value_dim) // group
    member = member_ref[0]
    for c, chunk in enumerate(chunks):
        for spot, j in enumerate(chunk):
            at = 0
            for ref, size in (
                (q_ref, key_dim), (k_ref, key_dim), (v_ref, value_dim), (g_ref, value_dim)
            ):
                whole[j, :, at : at + size] = ref[:, j * size : (j + 1) * size]
                at += size
            for k in range(group):
                start = pl.multiple_of((member ^ k) * share, 128)
                outs[c * group + k][:, spot * share : (spot + 1) * share] = whole[
                    j, :, pl.ds(start, share)
                ]


def pack(heads, chunks, group, member, tables):
    rows = tables[0].shape[0]
    width = sum(table.shape[1] for table in tables) // heads
    shapes = [(rows, len(chunk) * width // group) for chunk in chunks for _ in range(group)]
    flat = pl.pallas_call(
        lambda *refs: pack_kernel(heads, chunks, group, *refs),
        out_shape=[jax.ShapeDtypeStruct(shape, jnp.bfloat16) for shape in shapes],
        grid_spec=pltpu.PrefetchScalarGridSpec(
            num_scalar_prefetch=1,
            grid=(1,),
            in_specs=[pl.BlockSpec(table.shape, lambda i, *_: (0, 0)) for table in tables],
            out_specs=[pl.BlockSpec(shape, lambda i, *_: (0, 0)) for shape in shapes],
            scratch_shapes=[pltpu.VMEM((heads, rows, width), jnp.bfloat16)],
        ),
        name="pack",
    )(member, *tables)
    return [flat[c * group : (c + 1) * group] for c in range(len(chunks))]


def norm_kernel(low_ref, member_ref, own_ref, own_far_ref, side_ref, side_far_ref, out_ref):
    low = low_ref[0] == 0
    member = member_ref[0]
    half = own_ref.shape[1]
    blocks = 4
    for s, (near_ref, far_ref) in enumerate(((own_ref, own_far_ref), (side_ref, side_far_ref))):
        near = near_ref[...].astype(jnp.float32)
        far = far_ref[...].astype(jnp.float32)
        size = 2 * half
        center = (
            jnp.sum(near, axis=-1, keepdims=True) + jnp.sum(far, axis=-1, keepdims=True)
        ) / size
        near = near - center
        far = far - center
        spread = (
            jnp.sum(near * near, axis=-1, keepdims=True)
            + jnp.sum(far * far, axis=-1, keepdims=True)
        ) / size
        scale = lax.rsqrt(spread + 1e-05)
        near = (near * scale).astype(jnp.bfloat16)
        far = (far * scale).astype(jnp.bfloat16)
        pair = (jnp.where(low, near, far), jnp.where(low, far, near))
        for c in range(2 * half // 128):
            z, b = c // blocks, c % blocks
            start = pl.multiple_of((z * blocks + (member ^ b)) * 128, 128)
            at = c * 128
            piece = pair[at // half][:, at % half : at % half + 128]
            out_ref[s, :, pl.ds(start, 128)] = piece


def norm(low, member, own, own_far, side, side_far):
    rows, half = own.shape
    block = 64
    spec = pl.BlockSpec((block, half), lambda i, *_: (i, 0))
    return pl.pallas_call(
        norm_kernel,
        out_shape=jax.ShapeDtypeStruct((2, rows, 2 * half), jnp.bfloat16),
        grid_spec=pltpu.PrefetchScalarGridSpec(
            num_scalar_prefetch=2,
            grid=(rows // block,),
            in_specs=[spec] * 4,
            out_specs=pl.BlockSpec((2, block, 2 * half), lambda i, *_: (0, i, 0)),
        ),
        name="norm",
    )(low, member, own, own_far, side, side_far)


def project_kernel(zpos_ref, mine_ref, there_ref, *refs):
    count = (len(refs)) // 2
    pieces, outs = refs[:count], refs[count:]
    depth = pieces[0].shape[0]
    rows = mine_ref.shape[1]
    quarter = depth // 4

    def product(x_ref, swapped):
        total = None
        for step, piece in enumerate(pieces):
            shard = lax.rem(zpos_ref[0] + (count - step), count)
            start = pl.multiple_of(shard * depth, 128)
            table = piece[...]
            if swapped:
                order = (1, 0, 3, 2)
                table = jnp.concatenate(
                    [table[b * quarter : (b + 1) * quarter] for b in order], axis=0
                )
            left = x_ref[:, :, pl.ds(start, depth)].reshape(2 * rows, depth)
            term = jnp.dot(left, table, preferred_element_type=jnp.float32)
            total = term if total is None else total + term
        return total.astype(jnp.bfloat16)

    @pl.when(pl.program_id(0) == 0)
    def _():
        got = product(mine_ref, False)
        outs[0][...] = got[:rows]
        outs[2][...] = got[rows:]

    @pl.when(pl.program_id(0) == 1)
    def _():
        got = product(there_ref, True)
        outs[1][...] = got[:rows]
        outs[3][...] = got[rows:]


def project(zpos, mine, there, pieces):
    _, rows, size = mine.shape
    width = pieces[0].shape[1]
    whole = pl.BlockSpec(mine.shape, lambda i, z: (0, 0, 0))
    return pl.pallas_call(
        project_kernel,
        out_shape=[jax.ShapeDtypeStruct((rows, width), jnp.bfloat16)] * 4,
        grid_spec=pltpu.PrefetchScalarGridSpec(
            num_scalar_prefetch=1,
            grid=(2,),
            in_specs=[whole, whole]
            + [pl.BlockSpec(piece.shape, lambda i, z: (0, 0)) for piece in pieces],
            out_specs=[pl.BlockSpec((rows, width), lambda i, z: (0, 0))] * 4,
        ),
        cost_estimate=pl.CostEstimate(
            flops=8 * rows * width * size,
            bytes_accessed=2 * (4 * rows * size + size * width + 4 * rows * width),
            transcendentals=0,
        ),
        name="project",
    )(zpos, mine, there, *pieces)


GROUP = 8


def retain_kernel(
    head, key_dim, value_dim, count, do_hidden, do_update,
    to_ref, acc_ref, rate_ref, member_ref, *refs,
):
    parts, state_ref = refs[:count], refs[count]
    outs = refs[-(do_hidden + do_update) :]
    draft = parts[0].shape[0] // GROUP
    rows = draft * GROUP
    log_rate = rate_ref[head]
    member = member_ref[0]
    mix = jnp.concatenate(canonical(member, [part[...] for part in parts]), axis=1)
    base = pl.program_id(0) * GROUP
    query = mix[:, :key_dim]
    keys = mix[:, key_dim : 2 * key_dim] * jnp.bfloat16(key_dim**-0.5)
    values = mix[:, 2 * key_dim : 2 * key_dim + value_dim]
    states = [state_ref[r, 0] for r in range(GROUP)]
    span = [slice(r * draft, (r + 1) * draft) for r in range(GROUP)]
    if do_hidden:
        gate = mix[:, 2 * key_dim + value_dim :].astype(jnp.float32)
        shift = draft.bit_length() - 1
        t_pos = lax.broadcasted_iota(jnp.int32, (rows, rows), 0)
        s_pos = lax.broadcasted_iota(jnp.int32, (rows, rows), 1)
        away = t_pos - s_pos
        inside_draft = (away >= 0) & (t_pos >> shift == s_pos >> shift)
        mask = jnp.where(
            inside_draft, jnp.exp(jnp.maximum(away, 0).astype(jnp.float32) * log_rate), 0.0
        )
        after = (lax.broadcasted_iota(jnp.int32, (rows, value_dim), 0) & (draft - 1)) + 1
        fade = jnp.exp(after.astype(jnp.float32) * log_rate)
        scores = lax.dot_general(
            query, keys, (((1,), (1,)), ((), ())), preferred_element_type=jnp.float32
        )
        carried = jnp.concatenate(
            [
                jnp.dot(query[span[r]], states[r], preferred_element_type=jnp.float32)
                for r in range(GROUP)
            ],
            axis=0,
        )
        weights = (scores * mask).astype(jnp.bfloat16)
        inside = jnp.dot(weights, values, preferred_element_type=jnp.float32)
        mixture = layer_norm(inside + carried * fade)
        answer = (jax.nn.silu(gate) * mixture).astype(jnp.bfloat16)
        for r in range(GROUP):
            outs[0][to_ref[base + r]] = answer[span[r]]
    if do_update:
        spot = lax.broadcasted_iota(jnp.int32, (draft, key_dim), 0)
        for r in range(GROUP):
            taken = acc_ref[base + r]
            left = jnp.maximum(taken - 1 - spot, 0).astype(jnp.float32)
            scale = jnp.where(spot < taken, jnp.exp(left * log_rate), 0.0)
            kept = (keys[span[r]].astype(jnp.float32) * scale).astype(jnp.bfloat16)
            fresh = lax.dot_general(
                kept, values[span[r]], (((0,), (0,)), ((), ())), preferred_element_type=jnp.float32
            )
            fade = jnp.exp(
                jnp.full((8, value_dim), taken.astype(jnp.float32) * log_rate, jnp.float32)
            )[:1]
            outs[-1][r, 0] = (fresh + fade * states[r].astype(jnp.float32)).astype(jnp.bfloat16)


def retain(head, at, spot, width, do_hidden, do_update, scalars, parts, state, answers, states):
    rows, _, key_dim, value_dim = state.shape
    draft = parts[0].shape[0] // rows
    share = 2 * (key_dim + value_dim) // len(parts)
    state_spec = pl.BlockSpec((GROUP, 1, key_dim, value_dim), lambda i, *_: (i, head, 0, 0))
    out_shape, out_specs, earlier = [], [], []
    if do_hidden:
        out_shape.append(jax.ShapeDtypeStruct((rows, draft, width * value_dim), jnp.bfloat16))
        out_specs.append(pl.BlockSpec((rows, draft, value_dim), lambda i, *_: (0, 0, spot)))
        earlier.append(answers)
    if do_update:
        out_shape.append(jax.ShapeDtypeStruct(state.shape, jnp.bfloat16))
        out_specs.append(state_spec)
        earlier.append(states)
    first = len(scalars) + len(parts) + 1
    more, aliases = [], {}
    for out, one in enumerate(earlier):
        if one is not None:
            aliases[first + len(more)] = out
            more.append(one)
    return pl.pallas_call(
        lambda *refs: retain_kernel(
            head, key_dim, value_dim, len(parts), do_hidden, do_update, *refs
        ),
        out_shape=out_shape,
        grid_spec=pltpu.PrefetchScalarGridSpec(
            num_scalar_prefetch=len(scalars),
            grid=(rows // GROUP,),
            in_specs=[
                pl.BlockSpec((GROUP * draft, share), lambda i, *_: (i, at)) for _ in parts
            ]
            + [state_spec]
            + [pl.BlockSpec(memory_space=pl.ANY) for _ in more],
            out_specs=out_specs,
        ),
        input_output_aliases=aliases,
        cost_estimate=pl.CostEstimate(
            flops=2 * rows * draft * key_dim * value_dim * 8,
            bytes_accessed=2 * rows * key_dim * value_dim * (1 + do_update),
            transcendentals=0,
        ),
        name="retain",
    )(*scalars, *parts, state, *more)


def settle_kernel(place_ref, *refs):
    parts, out_ref = refs[:-1], refs[-1]
    for s in range(parts[0].shape[0]):
        row = place_ref[s]
        at = 0
        for part in parts:
            out_ref[row, :, at : at + part.shape[2]] = part[s]
            at += part.shape[2]


def settle(place_of, parts):
    rows, draft, _ = parts[0].shape
    whole = (rows, draft, sum(part.shape[2] for part in parts))
    return pl.pallas_call(
        settle_kernel,
        out_shape=jax.ShapeDtypeStruct(whole, jnp.bfloat16),
        grid_spec=pltpu.PrefetchScalarGridSpec(
            num_scalar_prefetch=1,
            grid=(1,),
            in_specs=[pl.BlockSpec(part.shape, lambda i, *_: (0, 0, 0)) for part in parts],
            out_specs=pl.BlockSpec(whole, lambda i, *_: (0, 0, 0)),
        ),
        name="settle",
    )(place_of, *parts)


def canonical(member, pieces):
    pieces = list(pieces)
    bit = 1
    while bit < len(pieces):
        swap = (member & bit) != 0
        pieces = [jnp.where(swap, pieces[k ^ bit], pieces[k]) for k in range(len(pieces))]
        bit *= 2
    return pieces


def swap_perm(group, k):
    return [(z * group + m, z * group + (m ^ k)) for z in range(ZLEN) for m in range(group)]


def ring_perm(group, shift):
    return [
        (z * group + m, ((z + shift) % ZLEN) * group + m) for z in range(ZLEN) for m in range(group)
    ]


def fast_device(
    draft_ids, worker_slot, accepted, embedding, w_query, w_key, w_value, w_gate, old_state
):
    own_rows, draft = draft_ids.shape
    heads = old_state.shape[1]
    key_dim, value_dim = old_state.shape[2:]
    group = lax.axis_size("req") // ZLEN
    member = lax.axis_index("req") % group
    zpos = lax.axis_index("req") // group

    head_ids = (lax.axis_index("head") * heads + jnp.arange(heads, dtype=jnp.int32)).astype(
        jnp.float32
    )
    log_rate = jnp.log1p(-jnp.exp2(-5.0 - head_ids))

    me = member.reshape(1).astype(jnp.int32)
    where_z = zpos.reshape(1).astype(jnp.int32)
    low = lax.axis_index("head").reshape(1).astype(jnp.int32)
    target = worker_slot // own_rows
    scalars = (target, accepted, log_rate, me)

    chunks = ((0, 1), (2,), (3,))
    packed = pack(heads, chunks, group, me, (w_query, w_key, w_value, w_gate))

    def swaps(c):
        parts = [part if k == 0 else side(part, k) for k, part in enumerate(packed[c])]
        return jnp.concatenate(parts, axis=0)

    def up(piece):
        return lax.ppermute(piece, "req", ring_perm(group, 1))

    def down(piece):
        return lax.ppermute(piece, "req", ring_perm(group, -1))

    def side(rows, k):
        return lax.ppermute(rows, "req", swap_perm(group, k))

    def fence(*values):
        return lax.optimization_barrier(values)

    plane_a, plane_b = swaps(0), swaps(1)
    one_b = up(plane_b)
    first, finish, place_of = token_rows(
        draft_ids, worker_slot, embedding, asked=(plane_a, plane_b), found=(one_b,)
    )
    plane_c = swaps(2)
    one_a = up(plane_a)
    first, one_a = fence(first, one_a)
    half = finish(first)

    three_a = down(after(plane_a, half))
    other = lax.ppermute(half, "head", [(0, 1), (1, 0)])
    half_x = side(half, 2)
    half, other, half_x, three_a, plane_b, plane_c = fence(
        half, other, half_x, three_a, plane_b, plane_c
    )
    other_x = side(other, 2)
    two_a = up(after(one_a, other))
    other_x, two_a, one_b, plane_b = fence(other_x, two_a, one_b, plane_b)
    mine = norm(low, me, half, other, half_x, other_x)
    there = side(mine, 1)
    three_b = down(plane_b)
    two_b = up(one_b)
    mine, there = fence(mine, there)

    def hand_back(parts):
        return [part if k == 0 else side(part, k) for k, part in enumerate(parts)]

    def send(answer):
        return lax.all_to_all(answer, "req", split_axis=0, concat_axis=0, tiled=True)

    made_a = project(where_z, mine, there, (plane_a, one_a, two_a, three_a))
    made_a, two_b, three_b, plane_c = fence(made_a, two_b, three_b, plane_c)
    mix_a = hand_back(made_a)
    one_c, three_c = up(plane_c), down(plane_c)
    made_b = project(where_z, mine, there, (plane_b, one_b, two_b, three_b))
    made_b, one_c = fence(made_b, one_c)
    mix_b = hand_back(made_b)
    two_c = up(one_c)
    mix_a, three_c = fence(mix_a, three_c)
    ahead, new_state = retain(0, 0, 0, 2, True, True, scalars, mix_a, old_state, None, None)
    ahead, two_c, three_c, new_state = fence(ahead, two_c, three_c, new_state)
    made_c = project(where_z, mine, there, (plane_c, one_c, two_c, three_c))
    mix_a, made_c = fence(mix_a, made_c)
    mix_c = hand_back(made_c)
    ahead, new_state = retain(1, 1, 1, 2, True, True, scalars, mix_a, old_state, ahead, new_state)
    front = send(ahead)
    behind, new_state = retain(2, 0, 0, 2, True, True, scalars, mix_b, old_state, None, new_state)
    (behind,) = retain(3, 0, 1, 2, True, False, scalars, mix_c, old_state, behind, None)
    back = send(behind)
    (new_state,) = retain(3, 0, 0, 1, False, True, scalars, mix_c, old_state, None, new_state)
    return settle(place_of, [front, back]), new_state


def plain_device(
    draft_ids, worker_slot, accepted, embedding, w_query, w_key, w_value, w_gate, old_state
):
    own_rows, draft = draft_ids.shape
    tables = [
        lax.all_gather(table, "req", axis=0, tiled=True)
        for table in (w_query, w_key, w_value, w_gate)
    ]
    half, finish, place_of = token_rows(draft_ids, worker_slot, embedding)
    half = finish(half)
    tokens = lax.all_gather(half, "head", axis=1, tiled=True)
    normed = layer_norm(tokens.astype(jnp.float32)).astype(jnp.bfloat16)
    raw = [jnp.dot(normed, table, preferred_element_type=jnp.float32) for table in tables]
    raw[1] = raw[1] * old_state.shape[2] ** (-0.5)
    made = [one.astype(jnp.bfloat16).reshape(own_rows, draft, -1) for one in raw]
    heads = old_state.shape[1]
    head_ids = (lax.axis_index("head") * heads + jnp.arange(heads, dtype=jnp.int32)).astype(
        jnp.float32
    )
    answer, new_state = retention(*made, old_state, accepted, head_ids)
    width = lax.axis_size("req")
    target = worker_slot // own_rows
    ahead = jnp.zeros((width,) + answer.shape[1:], answer.dtype).at[target].set(answer)
    received = lax.all_to_all(ahead, "req", split_axis=0, concat_axis=0, tiled=True)
    mine = lax.axis_index("req")
    valid = lax.all_to_all(
        (target[None, :] == jnp.arange(width)[:, None]).any(axis=1).astype(jnp.int32)[:, None],
        "req", split_axis=0, concat_axis=0, tiled=True,
    )[:, 0]
    spot = jnp.where(valid > 0, place_of, own_rows)
    hidden = jnp.zeros_like(answer).at[spot].set(received, mode="drop")
    return hidden, new_state


def solution(mesh):
    width, head_width = mesh.shape["req"], mesh.shape["head"]
    fast = head_width == 2 and width == 16
    return jax.shard_map(
        fast_device if fast else plain_device,
        mesh=mesh,
        in_specs=(
            P("req", None),
            P("req"),
            P("req"),
            P("req", "head"),
            P("req", "head"),
            P("req", "head"),
            P("req", "head"),
            P("req", "head"),
            P("req", "head", None, None),
        ),
        out_specs=(P("req", None, "head"), P("req", "head", None, None)),
        check_vma=False,
    )
```

```python
import jax
import jax.numpy as jnp
from jax import lax
from jax.experimental import pallas as pl
from jax.experimental.pallas import tpu as pltpu
from jax.sharding import PartitionSpec as P

ZLEN = 4


def layer_norm(values):
    center = jnp.mean(values, axis=-1, keepdims=True)
    shifted = values - center
    spread = jnp.mean(shifted * shifted, axis=-1, keepdims=True)
    return shifted * lax.rsqrt(spread + 1e-05)


def retention(queries, keys_scaled, values_all, gates_all, start_state, counts_int, head_ids):
    row_count = queries.shape[0]
    draft_len = queries.shape[1]
    heads_dev = start_state.shape[1]
    key_dim = start_state.shape[2]
    value_dim = start_state.shape[3]
    query_heads = queries.reshape(row_count, draft_len, heads_dev, key_dim)
    key_heads = keys_scaled.reshape(row_count, draft_len, heads_dev, key_dim)
    value_heads = values_all.reshape(row_count, draft_len, heads_dev, value_dim)
    gate_heads = gates_all.reshape(row_count, draft_len, heads_dev, value_dim)
    decay_rate = 1.0 - jnp.exp2(-5.0 - head_ids)
    positions = jnp.arange(draft_len, dtype=jnp.float32)
    distance = positions[:, None] - positions[None, :]
    causal = distance >= 0.0
    decay_mask = jnp.where(
        causal[None], jnp.power(decay_rate[:, None, None], jnp.maximum(distance, 0.0)[None]), 0.0
    )
    scores = (
        jnp.einsum("nthk,nshk->nhts", query_heads, key_heads, preferred_element_type=jnp.float32)
        * decay_mask[None]
    )
    weights = scores.astype(jnp.bfloat16)
    inside_terms = jnp.einsum(
        "nhts,nshv->nthv", weights, value_heads, preferred_element_type=jnp.float32
    )
    state_terms = jnp.einsum(
        "nthk,nhkv->nthv", query_heads, start_state, preferred_element_type=jnp.float32
    )
    state_terms = (
        state_terms * jnp.power(decay_rate[None, :], positions[:, None] + 1.0)[None, :, :, None]
    )
    mixture = layer_norm(inside_terms + state_terms)
    hidden = (jax.nn.silu(gate_heads.astype(jnp.float32)) * mixture).astype(jnp.bfloat16)
    hidden = hidden.reshape(row_count, draft_len, heads_dev * value_dim)
    counts = counts_int.astype(jnp.float32)[:, None]
    remaining = jnp.maximum(counts - 1.0 - positions[None, :], 0.0)
    within = positions[None, :] < counts
    scale_rows = jnp.where(
        within[:, :, None], jnp.power(decay_rate[None, None, :], remaining[:, :, None]), 0.0
    )
    kept_keys = (key_heads.astype(jnp.float32) * scale_rows[..., None]).astype(jnp.bfloat16)
    updated = jnp.einsum(
        "nshk,nshv->nhkv", kept_keys, value_heads, preferred_element_type=jnp.float32
    )
    updated = updated + jnp.power(decay_rate[None, :], counts)[
        :, :, None, None
    ] * start_state.astype(jnp.float32)
    return (hidden, updated.astype(jnp.bfloat16))


def after(value, *needed):
    return lax.optimization_barrier((value, needed))[0]


class Asked:
    def __init__(self, draft_ids, worker_slot, embedding):
        self.embedding = embedding
        self.width = width = lax.axis_size("req")
        own_rows, draft_len = draft_ids.shape
        count = own_rows * draft_len
        vocab_rows, self.cols = embedding.shape
        self.cap = cap = -(-2 * count // width)
        lanes = -(-(cap + 2) // 128) * 128
        ids = draft_ids.reshape(count)
        self.holder = holder = ids // vocab_rows
        self.local = ids - holder * vocab_rows
        order = jnp.arange(count, dtype=jnp.int32)
        same = ids[:, None] == ids[None, :]
        first_at = jnp.min(jnp.where(same, order[None, :], count), axis=1)
        self.is_first = is_first = first_at == order
        peers = is_first[None, :] & (holder[:, None] == holder[None, :])
        self.rank = jnp.sum((peers & (order[None, :] < first_at[:, None])).astype(jnp.int32), axis=1)
        most = jnp.max(jnp.sum(peers.astype(jnp.int32), axis=1))
        own_rounds = (most + cap - 1) // cap
        target = worker_slot // own_rows
        place = worker_slot - target * own_rows
        to_target = target[None, :] == jnp.arange(width, dtype=jnp.int32)[:, None]
        place_for = jnp.sum(jnp.where(to_target, place[None, :], 0), axis=1)
        self.table = jnp.concatenate(
            [
                self.requests(0),
                place_for[:, None],
                jnp.full((width, 1), own_rounds, jnp.int32),
                jnp.zeros((width, lanes - cap - 2), jnp.int32),
            ],
            axis=1,
        )

    def requests(self, turn):
        cap = self.cap
        now = self.is_first & (self.rank // cap == turn)
        spot = jnp.where(now, self.holder * cap + self.rank % cap, -1)
        hit = spot[None, :] == jnp.arange(self.width * cap, dtype=jnp.int32)[:, None]
        return jnp.sum(jnp.where(hit, self.local[None, :], 0), axis=1).reshape(self.width, cap)

    def rows_for(self, wanted, needed=None):
        rows = self.width * self.cap
        picked = jnp.take(self.embedding, wanted.reshape(rows), axis=0, mode="clip")
        if needed is not None:
            picked = after(picked, needed)
        got = trade(picked.reshape(self.width, self.cap, self.cols)).reshape(rows, self.cols)
        return jnp.take(got, self.holder * self.cap + self.rank % self.cap, axis=0, mode="clip")

    def fetch(self, asked=None, found=None):
        heard = trade(self.table)
        if asked is not None:
            heard = after(heard, asked)
        place_of = heard[:, self.cap]
        rounds = jnp.max(heard[:, self.cap + 1])
        first = self.rows_for(heard[:, : self.cap], found)

        def step(carry):
            turn, held = carry
            fresh = self.rows_for(trade(self.requests(turn)))
            return turn + 1, jnp.where((self.rank // self.cap == turn)[:, None], fresh, held)

        def finish(rows):
            return lax.while_loop(lambda carry: carry[0] < rounds, step, (jnp.int32(1), rows))[1]

        return first, finish, place_of


def trade(table):
    return lax.all_to_all(table, "req", split_axis=0, concat_axis=0, tiled=True)


BRIEF = pl.CostEstimate(flops=1, bytes_accessed=1, transcendentals=0)


def pack_kernel(heads, chunks, group, member_ref, q_ref, k_ref, v_ref, g_ref, *refs):
    outs, whole = refs[:-1], refs[-1]
    key_dim, value_dim = q_ref.shape[1] // heads, v_ref.shape[1] // heads
    share = 2 * (key_dim + value_dim) // group
    member = member_ref[0]
    for c, chunk in enumerate(chunks):
        for spot, j in enumerate(chunk):
            at = 0
            for ref, size in (
                (q_ref, key_dim), (k_ref, key_dim), (v_ref, value_dim), (g_ref, value_dim)
            ):
                whole[j, :, at : at + size] = ref[:, j * size : (j + 1) * size]
                at += size
            for k in range(group):
                start = pl.multiple_of((member ^ k) * share, 128)
                outs[c * group + k][:, spot * share : (spot + 1) * share] = whole[
                    j, :, pl.ds(start, share)
                ]


def pack(heads, chunks, group, member, tables):
    rows = tables[0].shape[0]
    width = sum(table.shape[1] for table in tables) // heads
    shapes = [(rows, len(chunk) * width // group) for chunk in chunks for _ in range(group)]
    flat = pl.pallas_call(
        lambda *refs: pack_kernel(heads, chunks, group, *refs),
        out_shape=[jax.ShapeDtypeStruct(shape, jnp.bfloat16) for shape in shapes],
        grid_spec=pltpu.PrefetchScalarGridSpec(
            num_scalar_prefetch=1,
            grid=(1,),
            in_specs=[pl.BlockSpec(table.shape, lambda i, *_: (0, 0)) for table in tables],
            out_specs=[pl.BlockSpec(shape, lambda i, *_: (0, 0)) for shape in shapes],
            scratch_shapes=[pltpu.VMEM((heads, rows, width), jnp.bfloat16)],
        ),
        cost_estimate=BRIEF,
        name="pack",
    )(member, *tables)
    return [flat[c * group : (c + 1) * group] for c in range(len(chunks))]


def norm_kernel(low_ref, member_ref, own_ref, own_far_ref, side_ref, side_far_ref, out_ref):
    low = low_ref[0] == 0
    member = member_ref[0]
    half = own_ref.shape[1]
    blocks = 4
    for s, (near_ref, far_ref) in enumerate(((own_ref, own_far_ref), (side_ref, side_far_ref))):
        near = near_ref[...].astype(jnp.float32)
        far = far_ref[...].astype(jnp.float32)
        size = 2 * half
        center = (
            jnp.sum(near, axis=-1, keepdims=True) + jnp.sum(far, axis=-1, keepdims=True)
        ) / size
        near = near - center
        far = far - center
        spread = (
            jnp.sum(near * near, axis=-1, keepdims=True)
            + jnp.sum(far * far, axis=-1, keepdims=True)
        ) / size
        scale = lax.rsqrt(spread + 1e-05)
        near = (near * scale).astype(jnp.bfloat16)
        far = (far * scale).astype(jnp.bfloat16)
        pair = (jnp.where(low, near, far), jnp.where(low, far, near))
        for c in range(2 * half // 128):
            z, b = c // blocks, c % blocks
            start = pl.multiple_of((z * blocks + (member ^ b)) * 128, 128)
            at = c * 128
            piece = pair[at // half][:, at % half : at % half + 128]
            out_ref[s, :, pl.ds(start, 128)] = piece


def norm(low, member, own, own_far, side, side_far):
    rows, half = own.shape
    block = 64
    spec = pl.BlockSpec((block, half), lambda i, *_: (i, 0))
    return pl.pallas_call(
        norm_kernel,
        out_shape=jax.ShapeDtypeStruct((2, rows, 2 * half), jnp.bfloat16),
        grid_spec=pltpu.PrefetchScalarGridSpec(
            num_scalar_prefetch=2,
            grid=(rows // block,),
            in_specs=[spec] * 4,
            out_specs=pl.BlockSpec((2, block, 2 * half), lambda i, *_: (0, i, 0)),
        ),
        cost_estimate=BRIEF,
        name="norm",
    )(low, member, own, own_far, side, side_far)


def project_kernel(count, zpos_ref, mine_ref, there_ref, *refs):
    pieces, outs = refs[:count], refs[count:]
    rows, size = mine_ref.shape[1:]
    depth = size // ZLEN
    quarter = depth // 4
    share = outs[0].shape[1]

    def product(x_ref, swapped):
        total = None
        for step in range(ZLEN):
            if count == 1:
                table, start = pieces[0][step * depth : (step + 1) * depth], step * depth
            else:
                shard = lax.rem(zpos_ref[0] + (ZLEN - step), ZLEN)
                table, start = pieces[step][...], pl.multiple_of(shard * depth, 128)
            if swapped:
                order = (1, 0, 3, 2)
                table = jnp.concatenate(
                    [table[b * quarter : (b + 1) * quarter] for b in order], axis=0
                )
            left = x_ref[:, :, pl.ds(start, depth)].reshape(2 * rows, depth)
            term = jnp.dot(left, table, preferred_element_type=jnp.float32)
            total = term if total is None else total + term
        return total.astype(jnp.bfloat16)

    def keep(got, k):
        for spot in range(len(outs) // 4):
            for half in range(2):
                outs[spot * 4 + k + 2 * half][...] = got[
                    half * rows : (half + 1) * rows, spot * share : (spot + 1) * share
                ]

    @pl.when(pl.program_id(0) == 0)
    def _():
        keep(product(mine_ref, False), 0)

    @pl.when(pl.program_id(0) == 1)
    def _():
        keep(product(there_ref, True), 1)


def project(zpos, mine, there, pieces, count=1):
    _, rows, size = mine.shape
    width = pieces[0].shape[1]
    whole = pl.BlockSpec(mine.shape, lambda i, z: (0, 0, 0))
    shape = (rows, width // count)
    outs = pl.pallas_call(
        lambda *refs: project_kernel(len(pieces), *refs),
        out_shape=[jax.ShapeDtypeStruct(shape, jnp.bfloat16)] * (4 * count),
        grid_spec=pltpu.PrefetchScalarGridSpec(
            num_scalar_prefetch=1,
            grid=(2,),
            in_specs=[whole, whole]
            + [pl.BlockSpec(piece.shape, lambda i, z: (0, 0)) for piece in pieces],
            out_specs=[pl.BlockSpec(shape, lambda i, z: (0, 0))] * (4 * count),
        ),
        cost_estimate=BRIEF,
        name="project",
    )(zpos, mine, there, *pieces)
    return [outs[spot * 4 : spot * 4 + 4] for spot in range(count)]


GROUP = 8


def retain_kernel(
    head, key_dim, value_dim, count, do_hidden, do_update,
    to_ref, acc_ref, rate_ref, member_ref, *refs,
):
    parts, state_ref = refs[:count], refs[count]
    outs = refs[-(do_hidden + do_update) :]
    draft = parts[0].shape[0] // GROUP
    rows = draft * GROUP
    log_rate = rate_ref[head]
    member = member_ref[0]
    mix = jnp.concatenate(canonical(member, [part[...] for part in parts]), axis=1)
    base = pl.program_id(0) * GROUP
    query = mix[:, :key_dim]
    keys = mix[:, key_dim : 2 * key_dim] * jnp.bfloat16(key_dim**-0.5)
    values = mix[:, 2 * key_dim : 2 * key_dim + value_dim]
    states = [state_ref[r, 0] for r in range(GROUP)]
    span = [slice(r * draft, (r + 1) * draft) for r in range(GROUP)]
    if do_hidden:
        gate = mix[:, 2 * key_dim + value_dim :].astype(jnp.float32)
        shift = draft.bit_length() - 1
        t_pos = lax.broadcasted_iota(jnp.int32, (rows, rows), 0)
        s_pos = lax.broadcasted_iota(jnp.int32, (rows, rows), 1)
        away = t_pos - s_pos
        inside_draft = (away >= 0) & (t_pos >> shift == s_pos >> shift)
        mask = jnp.where(
            inside_draft, jnp.exp(jnp.maximum(away, 0).astype(jnp.float32) * log_rate), 0.0
        )
        after = (lax.broadcasted_iota(jnp.int32, (rows, value_dim), 0) & (draft - 1)) + 1
        fade = jnp.exp(after.astype(jnp.float32) * log_rate)
        scores = lax.dot_general(
            query, keys, (((1,), (1,)), ((), ())), preferred_element_type=jnp.float32
        )
        carried = jnp.concatenate(
            [
                jnp.dot(query[span[r]], states[r], preferred_element_type=jnp.float32)
                for r in range(GROUP)
            ],
            axis=0,
        )
        weights = (scores * mask).astype(jnp.bfloat16)
        inside = jnp.dot(weights, values, preferred_element_type=jnp.float32)
        mixture = layer_norm(inside + carried * fade)
        answer = (jax.nn.silu(gate) * mixture).astype(jnp.bfloat16)
        for r in range(GROUP):
            outs[0][to_ref[base + r]] = answer[span[r]]
    if do_update:
        spot = lax.broadcasted_iota(jnp.int32, (draft, key_dim), 0)
        for r in range(GROUP):
            taken = acc_ref[base + r]
            left = jnp.maximum(taken - 1 - spot, 0).astype(jnp.float32)
            scale = jnp.where(spot < taken, jnp.exp(left * log_rate), 0.0)
            kept = (keys[span[r]].astype(jnp.float32) * scale).astype(jnp.bfloat16)
            fresh = lax.dot_general(
                kept, values[span[r]], (((0,), (0,)), ((), ())), preferred_element_type=jnp.float32
            )
            fade = jnp.exp(
                jnp.full((8, value_dim), taken.astype(jnp.float32) * log_rate, jnp.float32)
            )[:1]
            outs[-1][r, 0] = (fresh + fade * states[r].astype(jnp.float32)).astype(jnp.bfloat16)


def retain(head, at, spot, width, do_hidden, do_update, scalars, parts, state, answers, states):
    rows, _, key_dim, value_dim = state.shape
    draft = parts[0].shape[0] // rows
    share = 2 * (key_dim + value_dim) // len(parts)
    state_spec = pl.BlockSpec((GROUP, 1, key_dim, value_dim), lambda i, *_: (i, head, 0, 0))
    out_shape, out_specs, earlier = [], [], []
    if do_hidden:
        out_shape.append(jax.ShapeDtypeStruct((rows, draft, width * value_dim), jnp.bfloat16))
        out_specs.append(pl.BlockSpec((rows, draft, value_dim), lambda i, *_: (0, 0, spot)))
        earlier.append(answers)
    if do_update:
        out_shape.append(jax.ShapeDtypeStruct(state.shape, jnp.bfloat16))
        out_specs.append(state_spec)
        earlier.append(states)
    first = len(scalars) + len(parts) + 1
    more, aliases = [], {}
    for out, one in enumerate(earlier):
        if one is not None:
            aliases[first + len(more)] = out
            more.append(one)
    return pl.pallas_call(
        lambda *refs: retain_kernel(
            head, key_dim, value_dim, len(parts), do_hidden, do_update, *refs
        ),
        out_shape=out_shape,
        grid_spec=pltpu.PrefetchScalarGridSpec(
            num_scalar_prefetch=len(scalars),
            grid=(rows // GROUP,),
            in_specs=[
                pl.BlockSpec((GROUP * draft, share), lambda i, *_: (i, at)) for _ in parts
            ]
            + [state_spec]
            + [pl.BlockSpec(memory_space=pl.ANY) for _ in more],
            out_specs=out_specs,
        ),
        input_output_aliases=aliases,
        cost_estimate=BRIEF,
        name="retain",
    )(*scalars, *parts, state, *more)


def settle_kernel(order, place_ref, *refs):
    parts, out_ref = refs[:-1], refs[-1]
    value_dim = out_ref.shape[2] // sum(len(heads) for heads in order)
    for s in range(parts[0].shape[0]):
        row = place_ref[s]
        for part, heads in zip(parts, order):
            for spot, j in enumerate(heads):
                out_ref[row, :, j * value_dim : (j + 1) * value_dim] = part[
                    s, :, spot * value_dim : (spot + 1) * value_dim
                ]


def settle(place_of, order, parts):
    rows, draft, _ = parts[0].shape
    whole = (rows, draft, sum(part.shape[2] for part in parts))
    return pl.pallas_call(
        lambda *refs: settle_kernel(order, *refs),
        out_shape=jax.ShapeDtypeStruct(whole, jnp.bfloat16),
        grid_spec=pltpu.PrefetchScalarGridSpec(
            num_scalar_prefetch=1,
            grid=(1,),
            in_specs=[pl.BlockSpec(part.shape, lambda i, *_: (0, 0, 0)) for part in parts],
            out_specs=pl.BlockSpec(whole, lambda i, *_: (0, 0, 0)),
        ),
        cost_estimate=BRIEF,
        name="settle",
    )(place_of, *parts)


def canonical(member, pieces):
    pieces = list(pieces)
    bit = 1
    while bit < len(pieces):
        swap = (member & bit) != 0
        pieces = [jnp.where(swap, pieces[k ^ bit], pieces[k]) for k in range(len(pieces))]
        bit *= 2
    return pieces


def swap_perm(group, k):
    return [(z * group + m, z * group + (m ^ k)) for z in range(ZLEN) for m in range(group)]


def ring_perm(group, shift):
    return [
        (z * group + m, ((z + shift) % ZLEN) * group + m) for z in range(ZLEN) for m in range(group)
    ]


def fast_device(
    draft_ids, worker_slot, accepted, embedding, w_query, w_key, w_value, w_gate, old_state
):
    own_rows, draft = draft_ids.shape
    heads = old_state.shape[1]
    key_dim, value_dim = old_state.shape[2:]
    group = lax.axis_size("req") // ZLEN
    member = lax.axis_index("req") % group
    zpos = lax.axis_index("req") // group

    head_ids = (lax.axis_index("head") * heads + jnp.arange(heads, dtype=jnp.int32)).astype(
        jnp.float32
    )
    log_rate = jnp.log1p(-jnp.exp2(-5.0 - head_ids))

    me = member.reshape(1).astype(jnp.int32)
    where_z = zpos.reshape(1).astype(jnp.int32)
    low = lax.axis_index("head").reshape(1).astype(jnp.int32)
    target = worker_slot // own_rows
    scalars = (target, accepted, log_rate, me)

    chunks = ((0, 1), (2,), (3,))
    tokens = Asked(draft_ids, worker_slot, embedding)
    packed = pack(heads, chunks, group, after(me, tokens.table), (w_query, w_key, w_value, w_gate))

    def swaps(c):
        parts = [part if k == 0 else side(part, k) for k, part in enumerate(packed[c])]
        return jnp.concatenate(parts, axis=0)

    def up(piece):
        return lax.ppermute(piece, "req", ring_perm(group, 1))

    def down(piece):
        return lax.ppermute(piece, "req", ring_perm(group, -1))

    def side(rows, k):
        return lax.ppermute(rows, "req", swap_perm(group, k))

    def fence(*values):
        return lax.optimization_barrier(values)

    def hand_back(parts):
        return [part if k == 0 else side(part, k) for k, part in enumerate(parts)]

    plane_b, plane_a = swaps(1), swaps(0)
    one_b, three_b = up(plane_b), down(plane_b)
    first, finish, place_of = tokens.fetch(asked=(plane_b,), found=(one_b,))
    first, three_b, plane_a = fence(first, three_b, plane_a)
    half = finish(first)

    two_b, one_a = up(after(one_b, half)), up(after(plane_a, half))
    other = lax.ppermute(half, "head", [(0, 1), (1, 0)])
    half_x = side(half, 2)
    half, other, half_x, two_b = fence(half, other, half_x, two_b)
    other_x = side(other, 2)
    three_a = down(after(plane_a, other))
    plane_c = swaps(2)
    other_x, one_a, plane_c = fence(other_x, one_a, plane_c)
    two_a = up(one_a)
    mine = norm(low, me, half, other, half_x, other_x)
    there = side(mine, 1)

    (made_b,) = project(where_z, mine, there, (plane_b, one_b, two_b, three_b))
    made_b, three_a = fence(made_b, three_a)
    mix_b, two_a, plane_c = fence(hand_back(made_b), two_a, plane_c)
    one_c, three_c = up(plane_c), down(plane_c)
    made_0, made_1 = project(where_z, mine, there, (plane_a, one_a, two_a, three_a), 2)
    mix_b, one_c, made_0, made_1 = fence(mix_b, one_c, made_0, made_1)
    mix_0, mix_1 = hand_back(made_0), hand_back(made_1)
    two_c = up(one_c)
    front, new_state = retain(2, 0, 0, 1, True, True, scalars, mix_b, old_state, None, None)
    front, mix_0, three_c = fence(front, mix_0, three_c)
    front = trade(front)
    (made_c,) = project(where_z, mine, there, (plane_c, one_c, two_c, three_c))
    mix_c = hand_back(made_c)
    mix_0, made_c = fence(mix_0, made_c)
    (back,) = retain(0, 0, 0, 3, True, False, scalars, mix_0, old_state, None, None)
    (back,) = retain(1, 0, 1, 3, True, False, scalars, mix_1, old_state, back, None)
    back, mix_c = fence(back, mix_c)
    (back,) = retain(3, 0, 2, 3, True, False, scalars, mix_c, old_state, back, None)
    back, mix_0, mix_1, mix_c = fence(back, mix_0, mix_1, mix_c)
    back = trade(back)
    for j, mix in ((0, mix_0), (1, mix_1), (3, mix_c)):
        (new_state,) = retain(j, 0, 0, 1, False, True, scalars, mix, old_state, None, new_state)
    return settle(place_of, ((2,), (0, 1, 3)), [front, back]), new_state


def plain_device(
    draft_ids, worker_slot, accepted, embedding, w_query, w_key, w_value, w_gate, old_state
):
    own_rows, draft = draft_ids.shape
    tables = [
        lax.all_gather(table, "req", axis=0, tiled=True)
        for table in (w_query, w_key, w_value, w_gate)
    ]
    half, finish, place_of = Asked(draft_ids, worker_slot, embedding).fetch()
    half = finish(half)
    tokens = lax.all_gather(half, "head", axis=1, tiled=True)
    normed = layer_norm(tokens.astype(jnp.float32)).astype(jnp.bfloat16)
    raw = [jnp.dot(normed, table, preferred_element_type=jnp.float32) for table in tables]
    raw[1] = raw[1] * old_state.shape[2] ** (-0.5)
    made = [one.astype(jnp.bfloat16).reshape(own_rows, draft, -1) for one in raw]
    heads = old_state.shape[1]
    head_ids = (lax.axis_index("head") * heads + jnp.arange(heads, dtype=jnp.int32)).astype(
        jnp.float32
    )
    answer, new_state = retention(*made, old_state, accepted, head_ids)
    width = lax.axis_size("req")
    target = worker_slot // own_rows
    ahead = jnp.zeros((width,) + answer.shape[1:], answer.dtype).at[target].set(answer)
    received = lax.all_to_all(ahead, "req", split_axis=0, concat_axis=0, tiled=True)
    mine = lax.axis_index("req")
    valid = lax.all_to_all(
        (target[None, :] == jnp.arange(width)[:, None]).any(axis=1).astype(jnp.int32)[:, None],
        "req", split_axis=0, concat_axis=0, tiled=True,
    )[:, 0]
    spot = jnp.where(valid > 0, place_of, own_rows)
    hidden = jnp.zeros_like(answer).at[spot].set(received, mode="drop")
    return hidden, new_state


def solution(mesh):
    width, head_width = mesh.shape["req"], mesh.shape["head"]
    fast = head_width == 2 and width == 16
    return jax.shard_map(
        fast_device if fast else plain_device,
        mesh=mesh,
        in_specs=(
            P("req", None),
            P("req"),
            P("req"),
            P("req", "head"),
            P("req", "head"),
            P("req", "head"),
            P("req", "head"),
            P("req", "head"),
            P("req", "head", None, None),
        ),
        out_specs=(P("req", None, "head"), P("req", "head", None, None)),
        check_vma=False,
    )
```

```python
import jax
import jax.numpy as jnp
from jax import lax
from jax.experimental import pallas as pl
from jax.experimental.pallas import tpu as pltpu
from jax.sharding import PartitionSpec as P

ZLEN = 4


def layer_norm(values):
    center = jnp.mean(values, axis=-1, keepdims=True)
    shifted = values - center
    spread = jnp.mean(shifted * shifted, axis=-1, keepdims=True)
    return shifted * lax.rsqrt(spread + 1e-05)


def retention(queries, keys_scaled, values_all, gates_all, start_state, counts_int, head_ids):
    row_count = queries.shape[0]
    draft_len = queries.shape[1]
    heads_dev = start_state.shape[1]
    key_dim = start_state.shape[2]
    value_dim = start_state.shape[3]
    query_heads = queries.reshape(row_count, draft_len, heads_dev, key_dim)
    key_heads = keys_scaled.reshape(row_count, draft_len, heads_dev, key_dim)
    value_heads = values_all.reshape(row_count, draft_len, heads_dev, value_dim)
    gate_heads = gates_all.reshape(row_count, draft_len, heads_dev, value_dim)
    decay_rate = 1.0 - jnp.exp2(-5.0 - head_ids)
    positions = jnp.arange(draft_len, dtype=jnp.float32)
    distance = positions[:, None] - positions[None, :]
    causal = distance >= 0.0
    decay_mask = jnp.where(
        causal[None], jnp.power(decay_rate[:, None, None], jnp.maximum(distance, 0.0)[None]), 0.0
    )
    scores = (
        jnp.einsum("nthk,nshk->nhts", query_heads, key_heads, preferred_element_type=jnp.float32)
        * decay_mask[None]
    )
    weights = scores.astype(jnp.bfloat16)
    inside_terms = jnp.einsum(
        "nhts,nshv->nthv", weights, value_heads, preferred_element_type=jnp.float32
    )
    state_terms = jnp.einsum(
        "nthk,nhkv->nthv", query_heads, start_state, preferred_element_type=jnp.float32
    )
    state_terms = (
        state_terms * jnp.power(decay_rate[None, :], positions[:, None] + 1.0)[None, :, :, None]
    )
    mixture = layer_norm(inside_terms + state_terms)
    hidden = (jax.nn.silu(gate_heads.astype(jnp.float32)) * mixture).astype(jnp.bfloat16)
    hidden = hidden.reshape(row_count, draft_len, heads_dev * value_dim)
    counts = counts_int.astype(jnp.float32)[:, None]
    remaining = jnp.maximum(counts - 1.0 - positions[None, :], 0.0)
    within = positions[None, :] < counts
    scale_rows = jnp.where(
        within[:, :, None], jnp.power(decay_rate[None, None, :], remaining[:, :, None]), 0.0
    )
    kept_keys = (key_heads.astype(jnp.float32) * scale_rows[..., None]).astype(jnp.bfloat16)
    updated = jnp.einsum(
        "nshk,nshv->nhkv", kept_keys, value_heads, preferred_element_type=jnp.float32
    )
    updated = updated + jnp.power(decay_rate[None, :], counts)[
        :, :, None, None
    ] * start_state.astype(jnp.float32)
    return (hidden, updated.astype(jnp.bfloat16))


def after(value, *needed):
    return lax.optimization_barrier((value, needed))[0]


class Asked:
    def __init__(self, draft_ids, worker_slot, embedding):
        self.embedding = embedding
        self.width = width = lax.axis_size("req")
        own_rows, draft_len = draft_ids.shape
        count = own_rows * draft_len
        vocab_rows, self.cols = embedding.shape
        self.cap = cap = -(-2 * count // width)
        lanes = -(-(cap + 2) // 128) * 128
        ids = draft_ids.reshape(count)
        self.holder = holder = ids // vocab_rows
        self.local = ids - holder * vocab_rows
        order = jnp.arange(count, dtype=jnp.int32)
        same = ids[:, None] == ids[None, :]
        first_at = jnp.min(jnp.where(same, order[None, :], count), axis=1)
        self.is_first = is_first = first_at == order
        peers = is_first[None, :] & (holder[:, None] == holder[None, :])
        self.rank = jnp.sum((peers & (order[None, :] < first_at[:, None])).astype(jnp.int32), axis=1)
        most = jnp.max(jnp.sum(peers.astype(jnp.int32), axis=1))
        own_rounds = (most + cap - 1) // cap
        target = worker_slot // own_rows
        place = worker_slot - target * own_rows
        to_target = target[None, :] == jnp.arange(width, dtype=jnp.int32)[:, None]
        place_for = jnp.sum(jnp.where(to_target, place[None, :], 0), axis=1)
        self.table = jnp.concatenate(
            [
                self.requests(0),
                place_for[:, None],
                jnp.full((width, 1), own_rounds, jnp.int32),
                jnp.zeros((width, lanes - cap - 2), jnp.int32),
            ],
            axis=1,
        )

    def requests(self, turn):
        cap = self.cap
        now = self.is_first & (self.rank // cap == turn)
        spot = jnp.where(now, self.holder * cap + self.rank % cap, -1)
        hit = spot[None, :] == jnp.arange(self.width * cap, dtype=jnp.int32)[:, None]
        return jnp.sum(jnp.where(hit, self.local[None, :], 0), axis=1).reshape(self.width, cap)

    def rows_for(self, wanted, needed=None):
        rows = self.width * self.cap
        picked = jnp.take(self.embedding, wanted.reshape(rows), axis=0, mode="clip")
        if needed is not None:
            picked = after(picked, needed)
        got = trade(picked.reshape(self.width, self.cap, self.cols)).reshape(rows, self.cols)
        return jnp.take(got, self.holder * self.cap + self.rank % self.cap, axis=0, mode="clip")

    def fetch(self, asked=None, found=None):
        heard = trade(self.table)
        if asked is not None:
            heard = after(heard, asked)
        place_of = heard[:, self.cap]
        rounds = jnp.max(heard[:, self.cap + 1])
        first = self.rows_for(heard[:, : self.cap], found)

        def step(carry):
            turn, held = carry
            fresh = self.rows_for(trade(self.requests(turn)))
            return turn + 1, jnp.where((self.rank // self.cap == turn)[:, None], fresh, held)

        def finish(rows):
            return lax.while_loop(lambda carry: carry[0] < rounds, step, (jnp.int32(1), rows))[1]

        return first, finish, place_of


def trade(table):
    return lax.all_to_all(table, "req", split_axis=0, concat_axis=0, tiled=True)


BRIEF = pl.CostEstimate(flops=1, bytes_accessed=1, transcendentals=0)


def pack_kernel(heads, chunks, group, member_ref, q_ref, k_ref, v_ref, g_ref, *refs):
    outs, whole = refs[:-1], refs[-1]
    key_dim, value_dim = q_ref.shape[1] // heads, v_ref.shape[1] // heads
    share = 2 * (key_dim + value_dim) // group
    member = member_ref[0]
    for c, chunk in enumerate(chunks):
        for spot, j in enumerate(chunk):
            at = 0
            for ref, size in (
                (q_ref, key_dim), (k_ref, key_dim), (v_ref, value_dim), (g_ref, value_dim)
            ):
                whole[j, :, at : at + size] = ref[:, j * size : (j + 1) * size]
                at += size
            for k in range(group):
                start = pl.multiple_of((member ^ k) * share, 128)
                outs[c * group + k][:, spot * share : (spot + 1) * share] = whole[
                    j, :, pl.ds(start, share)
                ]


def pack(heads, chunks, group, member, tables):
    rows = tables[0].shape[0]
    width = sum(table.shape[1] for table in tables) // heads
    shapes = [(rows, len(chunk) * width // group) for chunk in chunks for _ in range(group)]
    flat = pl.pallas_call(
        lambda *refs: pack_kernel(heads, chunks, group, *refs),
        out_shape=[jax.ShapeDtypeStruct(shape, jnp.bfloat16) for shape in shapes],
        grid_spec=pltpu.PrefetchScalarGridSpec(
            num_scalar_prefetch=1,
            grid=(1,),
            in_specs=[pl.BlockSpec(table.shape, lambda i, *_: (0, 0)) for table in tables],
            out_specs=[pl.BlockSpec(shape, lambda i, *_: (0, 0)) for shape in shapes],
            scratch_shapes=[pltpu.VMEM((heads, rows, width), jnp.bfloat16)],
        ),
        cost_estimate=BRIEF,
        name="pack",
    )(member, *tables)
    return [flat[c * group : (c + 1) * group] for c in range(len(chunks))]


def norm_kernel(low_ref, member_ref, own_ref, own_far_ref, side_ref, side_far_ref, out_ref):
    low = low_ref[0] == 0
    member = member_ref[0]
    half = own_ref.shape[1]
    blocks = 4
    for s, (near_ref, far_ref) in enumerate(((own_ref, own_far_ref), (side_ref, side_far_ref))):
        near = near_ref[...].astype(jnp.float32)
        far = far_ref[...].astype(jnp.float32)
        size = 2 * half
        center = (
            jnp.sum(near, axis=-1, keepdims=True) + jnp.sum(far, axis=-1, keepdims=True)
        ) / size
        near = near - center
        far = far - center
        spread = (
            jnp.sum(near * near, axis=-1, keepdims=True)
            + jnp.sum(far * far, axis=-1, keepdims=True)
        ) / size
        scale = lax.rsqrt(spread + 1e-05)
        near = (near * scale).astype(jnp.bfloat16)
        far = (far * scale).astype(jnp.bfloat16)
        pair = (jnp.where(low, near, far), jnp.where(low, far, near))
        for c in range(2 * half // 128):
            z, b = c // blocks, c % blocks
            start = pl.multiple_of((z * blocks + (member ^ b)) * 128, 128)
            at = c * 128
            piece = pair[at // half][:, at % half : at % half + 128]
            out_ref[s, :, pl.ds(start, 128)] = piece


def norm(low, member, own, own_far, side, side_far):
    rows, half = own.shape
    block = 64
    spec = pl.BlockSpec((block, half), lambda i, *_: (i, 0))
    return pl.pallas_call(
        norm_kernel,
        out_shape=jax.ShapeDtypeStruct((2, rows, 2 * half), jnp.bfloat16),
        grid_spec=pltpu.PrefetchScalarGridSpec(
            num_scalar_prefetch=2,
            grid=(rows // block,),
            in_specs=[spec] * 4,
            out_specs=pl.BlockSpec((2, block, 2 * half), lambda i, *_: (0, i, 0)),
        ),
        cost_estimate=BRIEF,
        name="norm",
    )(low, member, own, own_far, side, side_far)


def project_kernel(count, zpos_ref, mine_ref, there_ref, *refs):
    pieces, outs = refs[:count], refs[count:]
    rows, size = mine_ref.shape[1:]
    depth = size // ZLEN
    quarter = depth // 4
    share = outs[0].shape[1]

    def product(x_ref, swapped):
        total = None
        for step in range(ZLEN):
            if count == 1:
                table, start = pieces[0][step * depth : (step + 1) * depth], step * depth
            else:
                shard = lax.rem(zpos_ref[0] + (ZLEN - step), ZLEN)
                table, start = pieces[step][...], pl.multiple_of(shard * depth, 128)
            if swapped:
                order = (1, 0, 3, 2)
                table = jnp.concatenate(
                    [table[b * quarter : (b + 1) * quarter] for b in order], axis=0
                )
            left = x_ref[:, :, pl.ds(start, depth)].reshape(2 * rows, depth)
            term = jnp.dot(left, table, preferred_element_type=jnp.float32)
            total = term if total is None else total + term
        return total.astype(jnp.bfloat16)

    def keep(got, k):
        for spot in range(len(outs) // 4):
            for half in range(2):
                outs[spot * 4 + k + 2 * half][...] = got[
                    half * rows : (half + 1) * rows, spot * share : (spot + 1) * share
                ]

    keep(product(mine_ref, False), 0)
    keep(product(there_ref, True), 1)


def project(zpos, mine, there, pieces, count=1):
    _, rows, size = mine.shape
    width = pieces[0].shape[1]
    shape = (rows, width // count)
    held = pl.BlockSpec(memory_space=pltpu.VMEM)
    outs = pl.pallas_call(
        lambda *refs: project_kernel(len(pieces), *refs),
        out_shape=[jax.ShapeDtypeStruct(shape, jnp.bfloat16)] * (4 * count),
        in_specs=[pl.BlockSpec(memory_space=pltpu.SMEM)] + [held] * (2 + len(pieces)),
        out_specs=[held] * (4 * count),
        cost_estimate=BRIEF,
        name="project",
    )(zpos, mine, there, *pieces)
    return [outs[spot * 4 : spot * 4 + 4] for spot in range(count)]


GROUP = 8


def retain_kernel(
    head, key_dim, value_dim, count, do_hidden, do_update,
    to_ref, acc_ref, rate_ref, member_ref, *refs,
):
    parts, state_ref = refs[:count], refs[count]
    outs = refs[-(do_hidden + do_update) :]
    draft = parts[0].shape[0] // GROUP
    rows = draft * GROUP
    log_rate = rate_ref[head]
    member = member_ref[0]
    mix = jnp.concatenate(canonical(member, [part[...] for part in parts]), axis=1)
    base = pl.program_id(0) * GROUP
    query = mix[:, :key_dim]
    keys = mix[:, key_dim : 2 * key_dim] * jnp.bfloat16(key_dim**-0.5)
    values = mix[:, 2 * key_dim : 2 * key_dim + value_dim]
    states = [state_ref[r, 0] for r in range(GROUP)]
    span = [slice(r * draft, (r + 1) * draft) for r in range(GROUP)]
    if do_hidden:
        gate = mix[:, 2 * key_dim + value_dim :].astype(jnp.float32)
        shift = draft.bit_length() - 1
        t_pos = lax.broadcasted_iota(jnp.int32, (rows, rows), 0)
        s_pos = lax.broadcasted_iota(jnp.int32, (rows, rows), 1)
        away = t_pos - s_pos
        inside_draft = (away >= 0) & (t_pos >> shift == s_pos >> shift)
        mask = jnp.where(
            inside_draft, jnp.exp(jnp.maximum(away, 0).astype(jnp.float32) * log_rate), 0.0
        )
        after = (lax.broadcasted_iota(jnp.int32, (rows, value_dim), 0) & (draft - 1)) + 1
        fade = jnp.exp(after.astype(jnp.float32) * log_rate)
        scores = lax.dot_general(
            query, keys, (((1,), (1,)), ((), ())), preferred_element_type=jnp.float32
        )
        carried = jnp.concatenate(
            [
                jnp.dot(query[span[r]], states[r], preferred_element_type=jnp.float32)
                for r in range(GROUP)
            ],
            axis=0,
        )
        weights = (scores * mask).astype(jnp.bfloat16)
        inside = jnp.dot(weights, values, preferred_element_type=jnp.float32)
        mixture = layer_norm(inside + carried * fade)
        answer = (jax.nn.silu(gate) * mixture).astype(jnp.bfloat16)
        for r in range(GROUP):
            outs[0][to_ref[base + r]] = answer[span[r]]
    if do_update:
        spot = lax.broadcasted_iota(jnp.int32, (draft, key_dim), 0)
        for r in range(GROUP):
            taken = acc_ref[base + r]
            left = jnp.maximum(taken - 1 - spot, 0).astype(jnp.float32)
            scale = jnp.where(spot < taken, jnp.exp(left * log_rate), 0.0)
            kept = (keys[span[r]].astype(jnp.float32) * scale).astype(jnp.bfloat16)
            fresh = lax.dot_general(
                kept, values[span[r]], (((0,), (0,)), ((), ())), preferred_element_type=jnp.float32
            )
            fade = jnp.exp(
                jnp.full((8, value_dim), taken.astype(jnp.float32) * log_rate, jnp.float32)
            )[:1]
            outs[-1][r, 0] = (fresh + fade * states[r].astype(jnp.float32)).astype(jnp.bfloat16)


def retain(head, at, spot, width, do_hidden, do_update, scalars, parts, state, answers, states):
    rows, _, key_dim, value_dim = state.shape
    draft = parts[0].shape[0] // rows
    share = 2 * (key_dim + value_dim) // len(parts)
    state_spec = pl.BlockSpec((GROUP, 1, key_dim, value_dim), lambda i, *_: (i, head, 0, 0))
    out_shape, out_specs, earlier = [], [], []
    if do_hidden:
        out_shape.append(jax.ShapeDtypeStruct((rows, draft, width * value_dim), jnp.bfloat16))
        out_specs.append(pl.BlockSpec((rows, draft, value_dim), lambda i, *_: (0, 0, spot)))
        earlier.append(answers)
    if do_update:
        out_shape.append(jax.ShapeDtypeStruct(state.shape, jnp.bfloat16))
        out_specs.append(state_spec)
        earlier.append(states)
    first = len(scalars) + len(parts) + 1
    more, aliases = [], {}
    for out, one in enumerate(earlier):
        if one is not None:
            aliases[first + len(more)] = out
            more.append(one)
    return pl.pallas_call(
        lambda *refs: retain_kernel(
            head, key_dim, value_dim, len(parts), do_hidden, do_update, *refs
        ),
        out_shape=out_shape,
        grid_spec=pltpu.PrefetchScalarGridSpec(
            num_scalar_prefetch=len(scalars),
            grid=(rows // GROUP,),
            in_specs=[
                pl.BlockSpec((GROUP * draft, share), lambda i, *_: (i, at)) for _ in parts
            ]
            + [state_spec]
            + [pl.BlockSpec(memory_space=pl.ANY) for _ in more],
            out_specs=out_specs,
        ),
        input_output_aliases=aliases,
        cost_estimate=BRIEF,
        name="retain",
    )(*scalars, *parts, state, *more)


def settle_kernel(order, place_ref, *refs):
    parts, out_ref = refs[:-1], refs[-1]
    value_dim = out_ref.shape[2] // sum(len(heads) for heads in order)
    for s in range(parts[0].shape[0]):
        row = place_ref[s]
        for part, heads in zip(parts, order):
            for spot, j in enumerate(heads):
                out_ref[row, :, j * value_dim : (j + 1) * value_dim] = part[
                    s, :, spot * value_dim : (spot + 1) * value_dim
                ]


def settle(place_of, order, parts):
    rows, draft, _ = parts[0].shape
    whole = (rows, draft, sum(part.shape[2] for part in parts))
    return pl.pallas_call(
        lambda *refs: settle_kernel(order, *refs),
        out_shape=jax.ShapeDtypeStruct(whole, jnp.bfloat16),
        grid_spec=pltpu.PrefetchScalarGridSpec(
            num_scalar_prefetch=1,
            grid=(1,),
            in_specs=[pl.BlockSpec(part.shape, lambda i, *_: (0, 0, 0)) for part in parts],
            out_specs=pl.BlockSpec(whole, lambda i, *_: (0, 0, 0)),
        ),
        cost_estimate=BRIEF,
        name="settle",
    )(place_of, *parts)


def canonical(member, pieces):
    pieces = list(pieces)
    bit = 1
    while bit < len(pieces):
        swap = (member & bit) != 0
        pieces = [jnp.where(swap, pieces[k ^ bit], pieces[k]) for k in range(len(pieces))]
        bit *= 2
    return pieces


def swap_perm(group, k):
    return [(z * group + m, z * group + (m ^ k)) for z in range(ZLEN) for m in range(group)]


def ring_perm(group, shift):
    return [
        (z * group + m, ((z + shift) % ZLEN) * group + m) for z in range(ZLEN) for m in range(group)
    ]


def fast_device(
    draft_ids, worker_slot, accepted, embedding, w_query, w_key, w_value, w_gate, old_state
):
    own_rows, draft = draft_ids.shape
    heads = old_state.shape[1]
    key_dim, value_dim = old_state.shape[2:]
    group = lax.axis_size("req") // ZLEN
    member = lax.axis_index("req") % group
    zpos = lax.axis_index("req") // group

    head_ids = (lax.axis_index("head") * heads + jnp.arange(heads, dtype=jnp.int32)).astype(
        jnp.float32
    )
    log_rate = jnp.log1p(-jnp.exp2(-5.0 - head_ids))

    me = member.reshape(1).astype(jnp.int32)
    where_z = zpos.reshape(1).astype(jnp.int32)
    low = lax.axis_index("head").reshape(1).astype(jnp.int32)
    target = worker_slot // own_rows
    scalars = (target, accepted, log_rate, me)

    chunks = ((0, 1), (2,), (3,))
    tokens = Asked(draft_ids, worker_slot, embedding)
    packed = pack(heads, chunks, group, after(me, tokens.table), (w_query, w_key, w_value, w_gate))

    def swaps(c):
        parts = [part if k == 0 else side(part, k) for k, part in enumerate(packed[c])]
        return jnp.concatenate(parts, axis=0)

    def up(piece):
        return lax.ppermute(piece, "req", ring_perm(group, 1))

    def down(piece):
        return lax.ppermute(piece, "req", ring_perm(group, -1))

    def side(rows, k):
        return lax.ppermute(rows, "req", swap_perm(group, k))

    def fence(*values):
        return lax.optimization_barrier(values)

    def hand_back(parts):
        return [part if k == 0 else side(part, k) for k, part in enumerate(parts)]

    plane_b, plane_a = swaps(1), swaps(0)
    one_b, three_b = up(plane_b), down(plane_b)
    first, finish, place_of = tokens.fetch(asked=(plane_b,), found=(one_b, three_b))
    first, plane_a = fence(first, plane_a)
    half = finish(first)

    two_b, one_a = up(after(one_b, half)), up(after(plane_a, half))
    three_a = down(after(plane_a, half))
    other = lax.ppermute(half, "head", [(0, 1), (1, 0)])
    half_x = side(half, 2)
    half, other, half_x, two_b = fence(half, other, half_x, two_b)
    other_x = side(other, 2)
    plane_c = swaps(2)
    other_x, one_a, plane_c = fence(other_x, one_a, plane_c)
    mine = norm(low, me, half, other, half_x, other_x)
    mine, three_a, one_a = fence(mine, three_a, one_a)
    two_a = up(one_a)
    there = side(mine, 1)

    (made_b,) = project(where_z, mine, there, (plane_b, one_b, two_b, three_b))
    mix_b, two_a, plane_c = fence(hand_back(made_b), two_a, plane_c)
    one_c, three_c = up(plane_c), down(plane_c)
    (made_a,) = project(where_z, mine, there, (plane_a, one_a, two_a, three_a))
    mix_b, one_c, made_a = fence(mix_b, one_c, made_a)
    mix_a = hand_back(made_a)
    two_c = up(one_c)
    front, new_state = retain(2, 0, 0, 1, True, True, scalars, mix_b, old_state, None, None)
    front = trade(front)
    new_state, mix_a[2], three_c, two_c = fence(new_state, mix_a[2], three_c, two_c)
    (made_c,) = project(where_z, mine, there, (plane_c, one_c, two_c, three_c))
    mix_a, made_c = fence(mix_a, made_c)
    mix_c = hand_back(made_c)
    (back,) = retain(0, 0, 0, 3, True, False, scalars, mix_a, old_state, None, None)
    (back,) = retain(1, 1, 1, 3, True, False, scalars, mix_a, old_state, back, None)
    back, mix_c = fence(back, mix_c)
    (back,) = retain(3, 0, 2, 3, True, False, scalars, mix_c, old_state, back, None)
    back, mix_a, mix_c = fence(back, mix_a, mix_c)
    back = trade(back)
    for j, at, mix in ((0, 0, mix_a), (1, 1, mix_a), (3, 0, mix_c)):
        (new_state,) = retain(j, at, 0, 1, False, True, scalars, mix, old_state, None, new_state)
    return settle(place_of, ((2,), (0, 1, 3)), [front, back]), new_state


def plain_device(
    draft_ids, worker_slot, accepted, embedding, w_query, w_key, w_value, w_gate, old_state
):
    own_rows, draft = draft_ids.shape
    tables = [
        lax.all_gather(table, "req", axis=0, tiled=True)
        for table in (w_query, w_key, w_value, w_gate)
    ]
    half, finish, place_of = Asked(draft_ids, worker_slot, embedding).fetch()
    half = finish(half)
    tokens = lax.all_gather(half, "head", axis=1, tiled=True)
    normed = layer_norm(tokens.astype(jnp.float32)).astype(jnp.bfloat16)
    raw = [jnp.dot(normed, table, preferred_element_type=jnp.float32) for table in tables]
    raw[1] = raw[1] * old_state.shape[2] ** (-0.5)
    made = [one.astype(jnp.bfloat16).reshape(own_rows, draft, -1) for one in raw]
    heads = old_state.shape[1]
    head_ids = (lax.axis_index("head") * heads + jnp.arange(heads, dtype=jnp.int32)).astype(
        jnp.float32
    )
    answer, new_state = retention(*made, old_state, accepted, head_ids)
    width = lax.axis_size("req")
    target = worker_slot // own_rows
    ahead = jnp.zeros((width,) + answer.shape[1:], answer.dtype).at[target].set(answer)
    received = lax.all_to_all(ahead, "req", split_axis=0, concat_axis=0, tiled=True)
    mine = lax.axis_index("req")
    valid = lax.all_to_all(
        (target[None, :] == jnp.arange(width)[:, None]).any(axis=1).astype(jnp.int32)[:, None],
        "req", split_axis=0, concat_axis=0, tiled=True,
    )[:, 0]
    spot = jnp.where(valid > 0, place_of, own_rows)
    hidden = jnp.zeros_like(answer).at[spot].set(received, mode="drop")
    return hidden, new_state


def solution(mesh):
    width, head_width = mesh.shape["req"], mesh.shape["head"]
    fast = head_width == 2 and width == 16
    return jax.shard_map(
        fast_device if fast else plain_device,
        mesh=mesh,
        in_specs=(
            P("req", None),
            P("req"),
            P("req"),
            P("req", "head"),
            P("req", "head"),
            P("req", "head"),
            P("req", "head"),
            P("req", "head"),
            P("req", "head", None, None),
        ),
        out_specs=(P("req", None, "head"), P("req", "head", None, None)),
        check_vma=False,
    )
```

```python
import jax
import jax.numpy as jnp
from jax import lax
from jax.experimental import pallas as pl
from jax.experimental.pallas import tpu as pltpu
from jax.sharding import PartitionSpec as P

ZLEN = 4


def layer_norm(values):
    center = jnp.mean(values, axis=-1, keepdims=True)
    shifted = values - center
    spread = jnp.mean(shifted * shifted, axis=-1, keepdims=True)
    return shifted * lax.rsqrt(spread + 1e-05)


def retention(queries, keys_scaled, values_all, gates_all, start_state, counts_int, head_ids):
    row_count = queries.shape[0]
    draft_len = queries.shape[1]
    heads_dev = start_state.shape[1]
    key_dim = start_state.shape[2]
    value_dim = start_state.shape[3]
    query_heads = queries.reshape(row_count, draft_len, heads_dev, key_dim)
    key_heads = keys_scaled.reshape(row_count, draft_len, heads_dev, key_dim)
    value_heads = values_all.reshape(row_count, draft_len, heads_dev, value_dim)
    gate_heads = gates_all.reshape(row_count, draft_len, heads_dev, value_dim)
    decay_rate = 1.0 - jnp.exp2(-5.0 - head_ids)
    positions = jnp.arange(draft_len, dtype=jnp.float32)
    distance = positions[:, None] - positions[None, :]
    causal = distance >= 0.0
    decay_mask = jnp.where(
        causal[None], jnp.power(decay_rate[:, None, None], jnp.maximum(distance, 0.0)[None]), 0.0
    )
    scores = (
        jnp.einsum("nthk,nshk->nhts", query_heads, key_heads, preferred_element_type=jnp.float32)
        * decay_mask[None]
    )
    weights = scores.astype(jnp.bfloat16)
    inside_terms = jnp.einsum(
        "nhts,nshv->nthv", weights, value_heads, preferred_element_type=jnp.float32
    )
    state_terms = jnp.einsum(
        "nthk,nhkv->nthv", query_heads, start_state, preferred_element_type=jnp.float32
    )
    state_terms = (
        state_terms * jnp.power(decay_rate[None, :], positions[:, None] + 1.0)[None, :, :, None]
    )
    mixture = layer_norm(inside_terms + state_terms)
    hidden = (jax.nn.silu(gate_heads.astype(jnp.float32)) * mixture).astype(jnp.bfloat16)
    hidden = hidden.reshape(row_count, draft_len, heads_dev * value_dim)
    counts = counts_int.astype(jnp.float32)[:, None]
    remaining = jnp.maximum(counts - 1.0 - positions[None, :], 0.0)
    within = positions[None, :] < counts
    scale_rows = jnp.where(
        within[:, :, None], jnp.power(decay_rate[None, None, :], remaining[:, :, None]), 0.0
    )
    kept_keys = (key_heads.astype(jnp.float32) * scale_rows[..., None]).astype(jnp.bfloat16)
    updated = jnp.einsum(
        "nshk,nshv->nhkv", kept_keys, value_heads, preferred_element_type=jnp.float32
    )
    updated = updated + jnp.power(decay_rate[None, :], counts)[
        :, :, None, None
    ] * start_state.astype(jnp.float32)
    return (hidden, updated.astype(jnp.bfloat16))


def after(value, *needed):
    return lax.optimization_barrier((value, needed))[0]


class Asked:
    def __init__(self, draft_ids, worker_slot, embedding):
        self.embedding = embedding
        self.width = width = lax.axis_size("req")
        own_rows, draft_len = draft_ids.shape
        count = own_rows * draft_len
        vocab_rows, self.cols = embedding.shape
        self.cap = cap = -(-2 * count // width)
        lanes = -(-(cap + 2) // 128) * 128
        ids = draft_ids.reshape(count)
        self.holder = holder = ids // vocab_rows
        self.local = ids - holder * vocab_rows
        order = jnp.arange(count, dtype=jnp.int32)
        same = ids[:, None] == ids[None, :]
        first_at = jnp.min(jnp.where(same, order[None, :], count), axis=1)
        self.is_first = is_first = first_at == order
        peers = is_first[None, :] & (holder[:, None] == holder[None, :])
        self.rank = jnp.sum((peers & (order[None, :] < first_at[:, None])).astype(jnp.int32), axis=1)
        most = jnp.max(jnp.sum(peers.astype(jnp.int32), axis=1))
        own_rounds = (most + cap - 1) // cap
        target = worker_slot // own_rows
        place = worker_slot - target * own_rows
        to_target = target[None, :] == jnp.arange(width, dtype=jnp.int32)[:, None]
        place_for = jnp.sum(jnp.where(to_target, place[None, :], 0), axis=1)
        self.table = jnp.concatenate(
            [
                self.requests(0),
                place_for[:, None],
                jnp.full((width, 1), own_rounds, jnp.int32),
                jnp.zeros((width, lanes - cap - 2), jnp.int32),
            ],
            axis=1,
        )

    def requests(self, turn):
        cap = self.cap
        now = self.is_first & (self.rank // cap == turn)
        spot = jnp.where(now, self.holder * cap + self.rank % cap, -1)
        hit = spot[None, :] == jnp.arange(self.width * cap, dtype=jnp.int32)[:, None]
        return jnp.sum(jnp.where(hit, self.local[None, :], 0), axis=1).reshape(self.width, cap)

    def rows_for(self, wanted, needed=None):
        rows = self.width * self.cap
        picked = jnp.take(self.embedding, wanted.reshape(rows), axis=0, mode="clip")
        if needed is not None:
            picked = after(picked, needed)
        got = trade(picked.reshape(self.width, self.cap, self.cols)).reshape(rows, self.cols)
        return jnp.take(got, self.holder * self.cap + self.rank % self.cap, axis=0, mode="clip")

    def fetch(self, heard, found=None):
        place_of = heard[:, self.cap]
        rounds = jnp.max(heard[:, self.cap + 1])
        first = self.rows_for(heard[:, : self.cap], found)

        def step(carry):
            turn, held = carry
            fresh = self.rows_for(trade(self.requests(turn)))
            return turn + 1, jnp.where((self.rank // self.cap == turn)[:, None], fresh, held)

        def finish(rows):
            return lax.while_loop(lambda carry: carry[0] < rounds, step, (jnp.int32(1), rows))[1]

        return first, finish, place_of


def trade(table):
    return lax.all_to_all(table, "req", split_axis=0, concat_axis=0, tiled=True)


BRIEF = pl.CostEstimate(flops=1, bytes_accessed=1, transcendentals=0)


def pack_kernel(heads, chunks, group, member_ref, q_ref, k_ref, v_ref, g_ref, *refs):
    outs, whole = refs[:-1], refs[-1]
    key_dim, value_dim = q_ref.shape[1] // heads, v_ref.shape[1] // heads
    share = 2 * (key_dim + value_dim) // group
    member = member_ref[0]
    for c, chunk in enumerate(chunks):
        for spot, j in enumerate(chunk):
            at = 0
            for ref, size in (
                (q_ref, key_dim), (k_ref, key_dim), (v_ref, value_dim), (g_ref, value_dim)
            ):
                whole[j, :, at : at + size] = ref[:, j * size : (j + 1) * size]
                at += size
            for k in range(group):
                start = pl.multiple_of((member ^ k) * share, 128)
                outs[c * group + k][:, spot * share : (spot + 1) * share] = whole[
                    j, :, pl.ds(start, share)
                ]


def pack(heads, chunks, group, member, tables):
    rows = tables[0].shape[0]
    width = sum(table.shape[1] for table in tables) // heads
    shapes = [(rows, len(chunk) * width // group) for chunk in chunks for _ in range(group)]
    flat = pl.pallas_call(
        lambda *refs: pack_kernel(heads, chunks, group, *refs),
        out_shape=[jax.ShapeDtypeStruct(shape, jnp.bfloat16) for shape in shapes],
        grid_spec=pltpu.PrefetchScalarGridSpec(
            num_scalar_prefetch=1,
            grid=(1,),
            in_specs=[pl.BlockSpec(table.shape, lambda i, *_: (0, 0)) for table in tables],
            out_specs=[pl.BlockSpec(shape, lambda i, *_: (0, 0)) for shape in shapes],
            scratch_shapes=[pltpu.VMEM((heads, rows, width), jnp.bfloat16)],
        ),
        cost_estimate=BRIEF,
        name="pack",
    )(member, *tables)
    return [flat[c * group : (c + 1) * group] for c in range(len(chunks))]


def norm_kernel(low_ref, member_ref, own_ref, own_far_ref, side_ref, side_far_ref, out_ref):
    low = low_ref[0] == 0
    member = member_ref[0]
    half = own_ref.shape[1]
    blocks = 4
    for s, (near_ref, far_ref) in enumerate(((own_ref, own_far_ref), (side_ref, side_far_ref))):
        near = near_ref[...].astype(jnp.float32)
        far = far_ref[...].astype(jnp.float32)
        size = 2 * half
        center = (
            jnp.sum(near, axis=-1, keepdims=True) + jnp.sum(far, axis=-1, keepdims=True)
        ) / size
        near = near - center
        far = far - center
        spread = (
            jnp.sum(near * near, axis=-1, keepdims=True)
            + jnp.sum(far * far, axis=-1, keepdims=True)
        ) / size
        scale = lax.rsqrt(spread + 1e-05)
        near = (near * scale).astype(jnp.bfloat16)
        far = (far * scale).astype(jnp.bfloat16)
        pair = (jnp.where(low, near, far), jnp.where(low, far, near))
        for c in range(2 * half // 128):
            z, b = c // blocks, c % blocks
            start = pl.multiple_of((z * blocks + (member ^ b)) * 128, 128)
            at = c * 128
            piece = pair[at // half][:, at % half : at % half + 128]
            out_ref[s, :, pl.ds(start, 128)] = piece


def norm(low, member, own, own_far, side, side_far):
    rows, half = own.shape
    block = 64
    spec = pl.BlockSpec((block, half), lambda i, *_: (i, 0))
    return pl.pallas_call(
        norm_kernel,
        out_shape=jax.ShapeDtypeStruct((2, rows, 2 * half), jnp.bfloat16),
        grid_spec=pltpu.PrefetchScalarGridSpec(
            num_scalar_prefetch=2,
            grid=(rows // block,),
            in_specs=[spec] * 4,
            out_specs=pl.BlockSpec((2, block, 2 * half), lambda i, *_: (0, i, 0)),
        ),
        cost_estimate=BRIEF,
        name="norm",
    )(low, member, own, own_far, side, side_far)


def project_kernel(count, zpos_ref, mine_ref, there_ref, *refs):
    pieces, outs = refs[:count], refs[count:]
    rows, size = mine_ref.shape[1:]
    depth = size // ZLEN
    quarter = depth // 4
    share = outs[0].shape[1]

    def product(x_ref, swapped):
        total = None
        for step in range(ZLEN):
            if count == 1:
                table, start = pieces[0][step * depth : (step + 1) * depth], step * depth
            else:
                shard = lax.rem(zpos_ref[0] + (ZLEN - step), ZLEN)
                table, start = pieces[step][...], pl.multiple_of(shard * depth, 128)
            if swapped:
                order = (1, 0, 3, 2)
                table = jnp.concatenate(
                    [table[b * quarter : (b + 1) * quarter] for b in order], axis=0
                )
            left = x_ref[:, :, pl.ds(start, depth)].reshape(2 * rows, depth)
            term = jnp.dot(left, table, preferred_element_type=jnp.float32)
            total = term if total is None else total + term
        return total.astype(jnp.bfloat16)

    def keep(got, k):
        for spot in range(len(outs) // 4):
            for half in range(2):
                outs[spot * 4 + k + 2 * half][...] = got[
                    half * rows : (half + 1) * rows, spot * share : (spot + 1) * share
                ]

    keep(product(mine_ref, False), 0)
    keep(product(there_ref, True), 1)


def project(zpos, mine, there, pieces, count=1):
    _, rows, size = mine.shape
    width = pieces[0].shape[1]
    shape = (rows, width // count)
    held = pl.BlockSpec(memory_space=pltpu.VMEM)
    outs = pl.pallas_call(
        lambda *refs: project_kernel(len(pieces), *refs),
        out_shape=[jax.ShapeDtypeStruct(shape, jnp.bfloat16)] * (4 * count),
        in_specs=[pl.BlockSpec(memory_space=pltpu.SMEM)] + [held] * (2 + len(pieces)),
        out_specs=[held] * (4 * count),
        cost_estimate=BRIEF,
        name="project",
    )(zpos, mine, there, *pieces)
    return [outs[spot * 4 : spot * 4 + 4] for spot in range(count)]


GROUP = 8


def retain_kernel(
    head, key_dim, value_dim, count, do_hidden, do_update,
    to_ref, acc_ref, rate_ref, member_ref, *refs,
):
    parts, state_ref = refs[:count], refs[count]
    outs = refs[-(do_hidden + do_update) :]
    draft = parts[0].shape[0] // GROUP
    rows = draft * GROUP
    log_rate = rate_ref[head]
    member = member_ref[0]
    mix = jnp.concatenate(canonical(member, [part[...] for part in parts]), axis=1)
    base = pl.program_id(0) * GROUP
    query = mix[:, :key_dim]
    keys = mix[:, key_dim : 2 * key_dim] * jnp.bfloat16(key_dim**-0.5)
    values = mix[:, 2 * key_dim : 2 * key_dim + value_dim]
    states = [state_ref[r, 0] for r in range(GROUP)]
    span = [slice(r * draft, (r + 1) * draft) for r in range(GROUP)]
    if do_hidden:
        gate = mix[:, 2 * key_dim + value_dim :].astype(jnp.float32)
        shift = draft.bit_length() - 1
        t_pos = lax.broadcasted_iota(jnp.int32, (rows, rows), 0)
        s_pos = lax.broadcasted_iota(jnp.int32, (rows, rows), 1)
        away = t_pos - s_pos
        inside_draft = (away >= 0) & (t_pos >> shift == s_pos >> shift)
        mask = jnp.where(
            inside_draft, jnp.exp(jnp.maximum(away, 0).astype(jnp.float32) * log_rate), 0.0
        )
        after = (lax.broadcasted_iota(jnp.int32, (rows, value_dim), 0) & (draft - 1)) + 1
        fade = jnp.exp(after.astype(jnp.float32) * log_rate)
        scores = lax.dot_general(
            query, keys, (((1,), (1,)), ((), ())), preferred_element_type=jnp.float32
        )
        carried = jnp.concatenate(
            [
                jnp.dot(query[span[r]], states[r], preferred_element_type=jnp.float32)
                for r in range(GROUP)
            ],
            axis=0,
        )
        weights = (scores * mask).astype(jnp.bfloat16)
        inside = jnp.dot(weights, values, preferred_element_type=jnp.float32)
        mixture = layer_norm(inside + carried * fade)
        answer = (jax.nn.silu(gate) * mixture).astype(jnp.bfloat16)
        for r in range(GROUP):
            outs[0][to_ref[base + r]] = answer[span[r]]
    if do_update:
        spot = lax.broadcasted_iota(jnp.int32, (draft, key_dim), 0)
        for r in range(GROUP):
            taken = acc_ref[base + r]
            left = jnp.maximum(taken - 1 - spot, 0).astype(jnp.float32)
            scale = jnp.where(spot < taken, jnp.exp(left * log_rate), 0.0)
            kept = (keys[span[r]].astype(jnp.float32) * scale).astype(jnp.bfloat16)
            fresh = lax.dot_general(
                kept, values[span[r]], (((0,), (0,)), ((), ())), preferred_element_type=jnp.float32
            )
            fade = jnp.exp(
                jnp.full((8, value_dim), taken.astype(jnp.float32) * log_rate, jnp.float32)
            )[:1]
            outs[-1][r, 0] = (fresh + fade * states[r].astype(jnp.float32)).astype(jnp.bfloat16)


def retain(head, at, spot, width, do_hidden, do_update, scalars, parts, state, answers, states):
    rows, _, key_dim, value_dim = state.shape
    draft = parts[0].shape[0] // rows
    share = 2 * (key_dim + value_dim) // len(parts)
    state_spec = pl.BlockSpec((GROUP, 1, key_dim, value_dim), lambda i, *_: (i, head, 0, 0))
    out_shape, out_specs, earlier = [], [], []
    if do_hidden:
        out_shape.append(jax.ShapeDtypeStruct((rows, draft, width * value_dim), jnp.bfloat16))
        out_specs.append(pl.BlockSpec((rows, draft, value_dim), lambda i, *_: (0, 0, spot)))
        earlier.append(answers)
    if do_update:
        out_shape.append(jax.ShapeDtypeStruct(state.shape, jnp.bfloat16))
        out_specs.append(state_spec)
        earlier.append(states)
    first = len(scalars) + len(parts) + 1
    more, aliases = [], {}
    for out, one in enumerate(earlier):
        if one is not None:
            aliases[first + len(more)] = out
            more.append(one)
    return pl.pallas_call(
        lambda *refs: retain_kernel(
            head, key_dim, value_dim, len(parts), do_hidden, do_update, *refs
        ),
        out_shape=out_shape,
        grid_spec=pltpu.PrefetchScalarGridSpec(
            num_scalar_prefetch=len(scalars),
            grid=(rows // GROUP,),
            in_specs=[
                pl.BlockSpec((GROUP * draft, share), lambda i, *_: (i, at)) for _ in parts
            ]
            + [state_spec]
            + [pl.BlockSpec(memory_space=pl.ANY) for _ in more],
            out_specs=out_specs,
        ),
        input_output_aliases=aliases,
        cost_estimate=BRIEF,
        name="retain",
    )(*scalars, *parts, state, *more)


def settle_kernel(order, place_ref, *refs):
    parts, out_ref = refs[:-1], refs[-1]
    value_dim = out_ref.shape[2] // sum(len(heads) for heads in order)
    for s in range(parts[0].shape[0]):
        row = place_ref[s]
        for part, heads in zip(parts, order):
            for spot, j in enumerate(heads):
                out_ref[row, :, j * value_dim : (j + 1) * value_dim] = part[
                    s, :, spot * value_dim : (spot + 1) * value_dim
                ]


def settle(place_of, order, parts):
    rows, draft, _ = parts[0].shape
    whole = (rows, draft, sum(part.shape[2] for part in parts))
    return pl.pallas_call(
        lambda *refs: settle_kernel(order, *refs),
        out_shape=jax.ShapeDtypeStruct(whole, jnp.bfloat16),
        grid_spec=pltpu.PrefetchScalarGridSpec(
            num_scalar_prefetch=1,
            grid=(1,),
            in_specs=[pl.BlockSpec(part.shape, lambda i, *_: (0, 0, 0)) for part in parts],
            out_specs=pl.BlockSpec(whole, lambda i, *_: (0, 0, 0)),
        ),
        cost_estimate=BRIEF,
        name="settle",
    )(place_of, *parts)


def canonical(member, pieces):
    pieces = list(pieces)
    bit = 1
    while bit < len(pieces):
        swap = (member & bit) != 0
        pieces = [jnp.where(swap, pieces[k ^ bit], pieces[k]) for k in range(len(pieces))]
        bit *= 2
    return pieces


def swap_perm(group, k):
    return [(z * group + m, z * group + (m ^ k)) for z in range(ZLEN) for m in range(group)]


def ring_perm(group, shift):
    return [
        (z * group + m, ((z + shift) % ZLEN) * group + m) for z in range(ZLEN) for m in range(group)
    ]


def fast_device(
    draft_ids, worker_slot, accepted, embedding, w_query, w_key, w_value, w_gate, old_state
):
    own_rows, draft = draft_ids.shape
    heads = old_state.shape[1]
    key_dim, value_dim = old_state.shape[2:]
    group = lax.axis_size("req") // ZLEN
    member = lax.axis_index("req") % group
    zpos = lax.axis_index("req") // group

    head_ids = (lax.axis_index("head") * heads + jnp.arange(heads, dtype=jnp.int32)).astype(
        jnp.float32
    )
    log_rate = jnp.log1p(-jnp.exp2(-5.0 - head_ids))

    me = member.reshape(1).astype(jnp.int32)
    where_z = zpos.reshape(1).astype(jnp.int32)
    low = lax.axis_index("head").reshape(1).astype(jnp.int32)
    target = worker_slot // own_rows
    scalars = (target, accepted, log_rate, me)

    chunks = ((0, 1), (2,), (3,))
    tokens = Asked(draft_ids, worker_slot, embedding)
    packed = pack(heads, chunks, group, after(me, tokens.table), (w_query, w_key, w_value, w_gate))

    def swaps(c):
        parts = [part if k == 0 else side(part, k) for k, part in enumerate(packed[c])]
        return jnp.concatenate(parts, axis=0)

    def up(piece):
        return lax.ppermute(piece, "req", ring_perm(group, 1))

    def down(piece):
        return lax.ppermute(piece, "req", ring_perm(group, -1))

    def side(rows, k):
        return lax.ppermute(rows, "req", swap_perm(group, k))

    def fence(*values):
        return lax.optimization_barrier(values)

    def hand_back(parts):
        return [part if k == 0 else side(part, k) for k, part in enumerate(parts)]

    plane_b, plane_a = swaps(1), swaps(0)
    one_b, three_b = up(plane_b), down(plane_b)
    heard = after(trade(tokens.table), plane_b)
    two_b = up(after(one_b, heard))
    first, finish, place_of = tokens.fetch(heard, found=(three_b, two_b))
    first, plane_a = fence(first, plane_a)
    half = finish(first)

    one_a = up(after(plane_a, half))
    three_a = down(after(plane_a, half))
    other = lax.ppermute(half, "head", [(0, 1), (1, 0)])
    half_x = side(half, 2)
    half, other, half_x = fence(half, other, half_x)
    other_x = side(other, 2)
    plane_c = swaps(2)
    other_x, one_a, plane_c = fence(other_x, one_a, plane_c)
    mine = norm(low, me, half, other, half_x, other_x)
    mine, three_a, one_a = fence(mine, three_a, one_a)
    two_a = up(one_a)
    there = side(mine, 1)

    (made_b,) = project(where_z, mine, there, (plane_b, one_b, two_b, three_b))
    mix_b, two_a, plane_c = fence(hand_back(made_b), two_a, plane_c)
    one_c, three_c = up(plane_c), down(plane_c)
    (made_a,) = project(where_z, mine, there, (plane_a, one_a, two_a, three_a))
    mix_b, one_c, made_a = fence(mix_b, one_c, made_a)
    mix_a = hand_back(made_a)
    two_c = up(one_c)
    front, new_state = retain(2, 0, 0, 1, True, True, scalars, mix_b, old_state, None, None)
    front = trade(front)
    new_state, mix_a[2], three_c, two_c = fence(new_state, mix_a[2], three_c, two_c)
    (made_c,) = project(where_z, mine, there, (plane_c, one_c, two_c, three_c))
    mix_a, made_c = fence(mix_a, made_c)
    mix_c = hand_back(made_c)
    (back,) = retain(0, 0, 0, 3, True, False, scalars, mix_a, old_state, None, None)
    (back,) = retain(1, 1, 1, 3, True, False, scalars, mix_a, old_state, back, None)
    back, mix_c = fence(back, mix_c)
    (back,) = retain(3, 0, 2, 3, True, False, scalars, mix_c, old_state, back, None)
    back, mix_a, mix_c = fence(back, mix_a, mix_c)
    back = trade(back)
    for j, at, mix in ((0, 0, mix_a), (1, 1, mix_a), (3, 0, mix_c)):
        (new_state,) = retain(j, at, 0, 1, False, True, scalars, mix, old_state, None, new_state)
    return settle(place_of, ((2,), (0, 1, 3)), [front, back]), new_state


def plain_device(
    draft_ids, worker_slot, accepted, embedding, w_query, w_key, w_value, w_gate, old_state
):
    own_rows, draft = draft_ids.shape
    tables = [
        lax.all_gather(table, "req", axis=0, tiled=True)
        for table in (w_query, w_key, w_value, w_gate)
    ]
    asked = Asked(draft_ids, worker_slot, embedding)
    half, finish, place_of = asked.fetch(trade(asked.table))
    half = finish(half)
    tokens = lax.all_gather(half, "head", axis=1, tiled=True)
    normed = layer_norm(tokens.astype(jnp.float32)).astype(jnp.bfloat16)
    raw = [jnp.dot(normed, table, preferred_element_type=jnp.float32) for table in tables]
    raw[1] = raw[1] * old_state.shape[2] ** (-0.5)
    made = [one.astype(jnp.bfloat16).reshape(own_rows, draft, -1) for one in raw]
    heads = old_state.shape[1]
    head_ids = (lax.axis_index("head") * heads + jnp.arange(heads, dtype=jnp.int32)).astype(
        jnp.float32
    )
    answer, new_state = retention(*made, old_state, accepted, head_ids)
    width = lax.axis_size("req")
    target = worker_slot // own_rows
    ahead = jnp.zeros((width,) + answer.shape[1:], answer.dtype).at[target].set(answer)
    received = lax.all_to_all(ahead, "req", split_axis=0, concat_axis=0, tiled=True)
    mine = lax.axis_index("req")
    valid = lax.all_to_all(
        (target[None, :] == jnp.arange(width)[:, None]).any(axis=1).astype(jnp.int32)[:, None],
        "req", split_axis=0, concat_axis=0, tiled=True,
    )[:, 0]
    spot = jnp.where(valid > 0, place_of, own_rows)
    hidden = jnp.zeros_like(answer).at[spot].set(received, mode="drop")
    return hidden, new_state


def solution(mesh):
    width, head_width = mesh.shape["req"], mesh.shape["head"]
    fast = head_width == 2 and width == 16
    return jax.shard_map(
        fast_device if fast else plain_device,
        mesh=mesh,
        in_specs=(
            P("req", None),
            P("req"),
            P("req"),
            P("req", "head"),
            P("req", "head"),
            P("req", "head"),
            P("req", "head"),
            P("req", "head"),
            P("req", "head", None, None),
        ),
        out_specs=(P("req", None, "head"), P("req", "head", None, None)),
        check_vma=False,
    )
```

```python
import jax
import jax.numpy as jnp
from jax import lax
from jax.experimental import pallas as pl
from jax.experimental.pallas import tpu as pltpu
from jax.sharding import PartitionSpec as P

ZLEN = 4


def layer_norm(values):
    center = jnp.mean(values, axis=-1, keepdims=True)
    shifted = values - center
    spread = jnp.mean(shifted * shifted, axis=-1, keepdims=True)
    return shifted * lax.rsqrt(spread + 1e-05)


def retention(queries, keys_scaled, values_all, gates_all, start_state, counts_int, head_ids):
    row_count = queries.shape[0]
    draft_len = queries.shape[1]
    heads_dev = start_state.shape[1]
    key_dim = start_state.shape[2]
    value_dim = start_state.shape[3]
    query_heads = queries.reshape(row_count, draft_len, heads_dev, key_dim)
    key_heads = keys_scaled.reshape(row_count, draft_len, heads_dev, key_dim)
    value_heads = values_all.reshape(row_count, draft_len, heads_dev, value_dim)
    gate_heads = gates_all.reshape(row_count, draft_len, heads_dev, value_dim)
    decay_rate = 1.0 - jnp.exp2(-5.0 - head_ids)
    positions = jnp.arange(draft_len, dtype=jnp.float32)
    distance = positions[:, None] - positions[None, :]
    causal = distance >= 0.0
    decay_mask = jnp.where(
        causal[None], jnp.power(decay_rate[:, None, None], jnp.maximum(distance, 0.0)[None]), 0.0
    )
    scores = (
        jnp.einsum("nthk,nshk->nhts", query_heads, key_heads, preferred_element_type=jnp.float32)
        * decay_mask[None]
    )
    weights = scores.astype(jnp.bfloat16)
    inside_terms = jnp.einsum(
        "nhts,nshv->nthv", weights, value_heads, preferred_element_type=jnp.float32
    )
    state_terms = jnp.einsum(
        "nthk,nhkv->nthv", query_heads, start_state, preferred_element_type=jnp.float32
    )
    state_terms = (
        state_terms * jnp.power(decay_rate[None, :], positions[:, None] + 1.0)[None, :, :, None]
    )
    mixture = layer_norm(inside_terms + state_terms)
    hidden = (jax.nn.silu(gate_heads.astype(jnp.float32)) * mixture).astype(jnp.bfloat16)
    hidden = hidden.reshape(row_count, draft_len, heads_dev * value_dim)
    counts = counts_int.astype(jnp.float32)[:, None]
    remaining = jnp.maximum(counts - 1.0 - positions[None, :], 0.0)
    within = positions[None, :] < counts
    scale_rows = jnp.where(
        within[:, :, None], jnp.power(decay_rate[None, None, :], remaining[:, :, None]), 0.0
    )
    kept_keys = (key_heads.astype(jnp.float32) * scale_rows[..., None]).astype(jnp.bfloat16)
    updated = jnp.einsum(
        "nshk,nshv->nhkv", kept_keys, value_heads, preferred_element_type=jnp.float32
    )
    updated = updated + jnp.power(decay_rate[None, :], counts)[
        :, :, None, None
    ] * start_state.astype(jnp.float32)
    return (hidden, updated.astype(jnp.bfloat16))


def after(value, *needed):
    return lax.optimization_barrier((value, needed))[0]


class Asked:
    def __init__(self, draft_ids, worker_slot, embedding):
        self.embedding = embedding
        self.width = width = lax.axis_size("req")
        own_rows, draft_len = draft_ids.shape
        count = own_rows * draft_len
        vocab_rows, self.cols = embedding.shape
        self.cap = cap = -(-2 * count // width)
        lanes = -(-(cap + 2) // 128) * 128
        ids = draft_ids.reshape(count)
        self.holder = holder = ids // vocab_rows
        self.local = ids - holder * vocab_rows
        order = jnp.arange(count, dtype=jnp.int32)
        same = ids[:, None] == ids[None, :]
        first_at = jnp.min(jnp.where(same, order[None, :], count), axis=1)
        self.is_first = is_first = first_at == order
        peers = is_first[None, :] & (holder[:, None] == holder[None, :])
        self.rank = jnp.sum((peers & (order[None, :] < first_at[:, None])).astype(jnp.int32), axis=1)
        most = jnp.max(jnp.sum(peers.astype(jnp.int32), axis=1))
        own_rounds = (most + cap - 1) // cap
        target = worker_slot // own_rows
        place = worker_slot - target * own_rows
        to_target = target[None, :] == jnp.arange(width, dtype=jnp.int32)[:, None]
        place_for = jnp.sum(jnp.where(to_target, place[None, :], 0), axis=1)
        self.table = jnp.concatenate(
            [
                self.requests(0),
                place_for[:, None],
                jnp.full((width, 1), own_rounds, jnp.int32),
                jnp.zeros((width, lanes - cap - 2), jnp.int32),
            ],
            axis=1,
        )

    def requests(self, turn):
        cap = self.cap
        now = self.is_first & (self.rank // cap == turn)
        spot = jnp.where(now, self.holder * cap + self.rank % cap, -1)
        hit = spot[None, :] == jnp.arange(self.width * cap, dtype=jnp.int32)[:, None]
        return jnp.sum(jnp.where(hit, self.local[None, :], 0), axis=1).reshape(self.width, cap)

    def rows_for(self, wanted, needed=None):
        rows = self.width * self.cap
        picked = jnp.take(self.embedding, wanted.reshape(rows), axis=0, mode="clip")
        if needed is not None:
            picked = after(picked, needed)
        got = trade(picked.reshape(self.width, self.cap, self.cols)).reshape(rows, self.cols)
        return jnp.take(got, self.holder * self.cap + self.rank % self.cap, axis=0, mode="clip")

    def fetch(self, heard, found=None):
        place_of = heard[:, self.cap]
        rounds = jnp.max(heard[:, self.cap + 1])
        first = self.rows_for(heard[:, : self.cap], found)

        def step(carry):
            turn, held = carry
            fresh = self.rows_for(trade(self.requests(turn)))
            return turn + 1, jnp.where((self.rank // self.cap == turn)[:, None], fresh, held)

        def finish(rows):
            return lax.while_loop(lambda carry: carry[0] < rounds, step, (jnp.int32(1), rows))[1]

        return first, finish, place_of


def trade(table):
    return lax.all_to_all(table, "req", split_axis=0, concat_axis=0, tiled=True)


BRIEF = pl.CostEstimate(flops=1, bytes_accessed=1, transcendentals=0)


def pack_kernel(heads, chunks, group, member_ref, q_ref, k_ref, v_ref, g_ref, *refs):
    outs, whole = refs[:-1], refs[-1]
    key_dim, value_dim = q_ref.shape[1] // heads, v_ref.shape[1] // heads
    share = 2 * (key_dim + value_dim) // group
    member = member_ref[0]
    for c, chunk in enumerate(chunks):
        for spot, j in enumerate(chunk):
            at = 0
            for ref, size in (
                (q_ref, key_dim), (k_ref, key_dim), (v_ref, value_dim), (g_ref, value_dim)
            ):
                whole[j, :, at : at + size] = ref[:, j * size : (j + 1) * size]
                at += size
            for k in range(group):
                start = pl.multiple_of((member ^ k) * share, 128)
                outs[c * group + k][:, spot * share : (spot + 1) * share] = whole[
                    j, :, pl.ds(start, share)
                ]


def pack(heads, chunks, group, member, tables):
    rows = tables[0].shape[0]
    width = sum(table.shape[1] for table in tables) // heads
    shapes = [(rows, len(chunk) * width // group) for chunk in chunks for _ in range(group)]
    flat = pl.pallas_call(
        lambda *refs: pack_kernel(heads, chunks, group, *refs),
        out_shape=[jax.ShapeDtypeStruct(shape, jnp.bfloat16) for shape in shapes],
        grid_spec=pltpu.PrefetchScalarGridSpec(
            num_scalar_prefetch=1,
            grid=(1,),
            in_specs=[pl.BlockSpec(table.shape, lambda i, *_: (0, 0)) for table in tables],
            out_specs=[pl.BlockSpec(shape, lambda i, *_: (0, 0)) for shape in shapes],
            scratch_shapes=[pltpu.VMEM((heads, rows, width), jnp.bfloat16)],
        ),
        cost_estimate=BRIEF,
        name="pack",
    )(member, *tables)
    return [flat[c * group : (c + 1) * group] for c in range(len(chunks))]


def norm_kernel(low_ref, member_ref, own_ref, own_far_ref, side_ref, side_far_ref, out_ref):
    low = low_ref[0] == 0
    member = member_ref[0]
    half = own_ref.shape[1]
    blocks = 4
    for s, (near_ref, far_ref) in enumerate(((own_ref, own_far_ref), (side_ref, side_far_ref))):
        near = near_ref[...].astype(jnp.float32)
        far = far_ref[...].astype(jnp.float32)
        size = 2 * half
        center = (
            jnp.sum(near, axis=-1, keepdims=True) + jnp.sum(far, axis=-1, keepdims=True)
        ) / size
        near = near - center
        far = far - center
        spread = (
            jnp.sum(near * near, axis=-1, keepdims=True)
            + jnp.sum(far * far, axis=-1, keepdims=True)
        ) / size
        scale = lax.rsqrt(spread + 1e-05)
        near = (near * scale).astype(jnp.bfloat16)
        far = (far * scale).astype(jnp.bfloat16)
        pair = (jnp.where(low, near, far), jnp.where(low, far, near))
        for c in range(2 * half // 128):
            z, b = c // blocks, c % blocks
            start = pl.multiple_of((z * blocks + (member ^ b)) * 128, 128)
            at = c * 128
            piece = pair[at // half][:, at % half : at % half + 128]
            out_ref[s, :, pl.ds(start, 128)] = piece


def norm(low, member, own, own_far, side, side_far):
    rows, half = own.shape
    block = 64
    spec = pl.BlockSpec((block, half), lambda i, *_: (i, 0))
    return pl.pallas_call(
        norm_kernel,
        out_shape=jax.ShapeDtypeStruct((2, rows, 2 * half), jnp.bfloat16),
        grid_spec=pltpu.PrefetchScalarGridSpec(
            num_scalar_prefetch=2,
            grid=(rows // block,),
            in_specs=[spec] * 4,
            out_specs=pl.BlockSpec((2, block, 2 * half), lambda i, *_: (0, i, 0)),
        ),
        cost_estimate=BRIEF,
        name="norm",
    )(low, member, own, own_far, side, side_far)


def project_kernel(count, zpos_ref, mine_ref, there_ref, *refs):
    pieces, outs = refs[:count], refs[count:]
    rows, size = mine_ref.shape[1:]
    depth = size // ZLEN
    quarter = depth // 4
    share = outs[0].shape[1]

    def product(x_ref, swapped):
        total = None
        for step in range(ZLEN):
            if count == 1:
                table, start = pieces[0][step * depth : (step + 1) * depth], step * depth
            else:
                shard = lax.rem(zpos_ref[0] + (ZLEN - step), ZLEN)
                table, start = pieces[step][...], pl.multiple_of(shard * depth, 128)
            if swapped:
                order = (1, 0, 3, 2)
                table = jnp.concatenate(
                    [table[b * quarter : (b + 1) * quarter] for b in order], axis=0
                )
            left = x_ref[:, :, pl.ds(start, depth)].reshape(2 * rows, depth)
            term = jnp.dot(left, table, preferred_element_type=jnp.float32)
            total = term if total is None else total + term
        return total.astype(jnp.bfloat16)

    def keep(got, k):
        for spot in range(len(outs) // 4):
            for half in range(2):
                outs[spot * 4 + k + 2 * half][...] = got[
                    half * rows : (half + 1) * rows, spot * share : (spot + 1) * share
                ]

    keep(product(mine_ref, False), 0)
    keep(product(there_ref, True), 1)


def project(zpos, mine, there, pieces, count=1):
    _, rows, size = mine.shape
    width = pieces[0].shape[1]
    shape = (rows, width // count)
    held = pl.BlockSpec(memory_space=pltpu.VMEM)
    outs = pl.pallas_call(
        lambda *refs: project_kernel(len(pieces), *refs),
        out_shape=[jax.ShapeDtypeStruct(shape, jnp.bfloat16)] * (4 * count),
        in_specs=[pl.BlockSpec(memory_space=pltpu.SMEM)] + [held] * (2 + len(pieces)),
        out_specs=[held] * (4 * count),
        cost_estimate=BRIEF,
        name="project",
    )(zpos, mine, there, *pieces)
    return [outs[spot * 4 : spot * 4 + 4] for spot in range(count)]


GROUP = 8


def retain_kernel(
    head, key_dim, value_dim, count, do_hidden, do_update,
    to_ref, acc_ref, rate_ref, member_ref, *refs,
):
    parts, state_ref = refs[:count], refs[count]
    outs = refs[-(do_hidden + do_update) :]
    draft = parts[0].shape[0] // GROUP
    rows = draft * GROUP
    log_rate = rate_ref[head]
    member = member_ref[0]
    mix = jnp.concatenate(canonical(member, [part[...] for part in parts]), axis=1)
    base = pl.program_id(0) * GROUP
    query = mix[:, :key_dim]
    keys = mix[:, key_dim : 2 * key_dim] * jnp.bfloat16(key_dim**-0.5)
    values = mix[:, 2 * key_dim : 2 * key_dim + value_dim]
    states = [state_ref[r, 0] for r in range(GROUP)]
    span = [slice(r * draft, (r + 1) * draft) for r in range(GROUP)]
    if do_hidden:
        gate = mix[:, 2 * key_dim + value_dim :].astype(jnp.float32)
        shift = draft.bit_length() - 1
        t_pos = lax.broadcasted_iota(jnp.int32, (rows, rows), 0)
        s_pos = lax.broadcasted_iota(jnp.int32, (rows, rows), 1)
        away = t_pos - s_pos
        inside_draft = (away >= 0) & (t_pos >> shift == s_pos >> shift)
        mask = jnp.where(
            inside_draft, jnp.exp(jnp.maximum(away, 0).astype(jnp.float32) * log_rate), 0.0
        )
        after = (lax.broadcasted_iota(jnp.int32, (rows, value_dim), 0) & (draft - 1)) + 1
        fade = jnp.exp(after.astype(jnp.float32) * log_rate)
        scores = lax.dot_general(
            query, keys, (((1,), (1,)), ((), ())), preferred_element_type=jnp.float32
        )
        carried = jnp.concatenate(
            [
                jnp.dot(query[span[r]], states[r], preferred_element_type=jnp.float32)
                for r in range(GROUP)
            ],
            axis=0,
        )
        weights = (scores * mask).astype(jnp.bfloat16)
        inside = jnp.dot(weights, values, preferred_element_type=jnp.float32)
        mixture = layer_norm(inside + carried * fade)
        answer = (jax.nn.silu(gate) * mixture).astype(jnp.bfloat16)
        for r in range(GROUP):
            outs[0][to_ref[base + r]] = answer[span[r]]
    if do_update:
        spot = lax.broadcasted_iota(jnp.int32, (draft, key_dim), 0)
        for r in range(GROUP):
            taken = acc_ref[base + r]
            left = jnp.maximum(taken - 1 - spot, 0).astype(jnp.float32)
            scale = jnp.where(spot < taken, jnp.exp(left * log_rate), 0.0)
            kept = (keys[span[r]].astype(jnp.float32) * scale).astype(jnp.bfloat16)
            fresh = lax.dot_general(
                kept, values[span[r]], (((0,), (0,)), ((), ())), preferred_element_type=jnp.float32
            )
            fade = jnp.exp(
                jnp.full((8, value_dim), taken.astype(jnp.float32) * log_rate, jnp.float32)
            )[:1]
            outs[-1][r, 0] = (fresh + fade * states[r].astype(jnp.float32)).astype(jnp.bfloat16)


def retain(head, at, spot, width, do_hidden, do_update, scalars, parts, state, answers, states):
    rows, _, key_dim, value_dim = state.shape
    draft = parts[0].shape[0] // rows
    share = 2 * (key_dim + value_dim) // len(parts)
    state_spec = pl.BlockSpec((GROUP, 1, key_dim, value_dim), lambda i, *_: (i, head, 0, 0))
    out_shape, out_specs, earlier = [], [], []
    if do_hidden:
        out_shape.append(jax.ShapeDtypeStruct((rows, draft, width * value_dim), jnp.bfloat16))
        out_specs.append(pl.BlockSpec((rows, draft, value_dim), lambda i, *_: (0, 0, spot)))
        earlier.append(answers)
    if do_update:
        out_shape.append(jax.ShapeDtypeStruct(state.shape, jnp.bfloat16))
        out_specs.append(state_spec)
        earlier.append(states)
    first = len(scalars) + len(parts) + 1
    more, aliases = [], {}
    for out, one in enumerate(earlier):
        if one is not None:
            aliases[first + len(more)] = out
            more.append(one)
    return pl.pallas_call(
        lambda *refs: retain_kernel(
            head, key_dim, value_dim, len(parts), do_hidden, do_update, *refs
        ),
        out_shape=out_shape,
        grid_spec=pltpu.PrefetchScalarGridSpec(
            num_scalar_prefetch=len(scalars),
            grid=(rows // GROUP,),
            in_specs=[
                pl.BlockSpec((GROUP * draft, share), lambda i, *_: (i, at)) for _ in parts
            ]
            + [state_spec]
            + [pl.BlockSpec(memory_space=pl.ANY) for _ in more],
            out_specs=out_specs,
        ),
        input_output_aliases=aliases,
        cost_estimate=BRIEF,
        name="retain",
    )(*scalars, *parts, state, *more)


def settle_kernel(order, place_ref, *refs):
    parts, out_ref = refs[:-1], refs[-1]
    value_dim = out_ref.shape[2] // sum(len(heads) for heads in order)
    for s in range(parts[0].shape[0]):
        row = place_ref[s]
        for part, heads in zip(parts, order):
            for spot, j in enumerate(heads):
                out_ref[row, :, j * value_dim : (j + 1) * value_dim] = part[
                    s, :, spot * value_dim : (spot + 1) * value_dim
                ]


def settle(place_of, order, parts):
    rows, draft, _ = parts[0].shape
    whole = (rows, draft, sum(part.shape[2] for part in parts))
    return pl.pallas_call(
        lambda *refs: settle_kernel(order, *refs),
        out_shape=jax.ShapeDtypeStruct(whole, jnp.bfloat16),
        grid_spec=pltpu.PrefetchScalarGridSpec(
            num_scalar_prefetch=1,
            grid=(1,),
            in_specs=[pl.BlockSpec(part.shape, lambda i, *_: (0, 0, 0)) for part in parts],
            out_specs=pl.BlockSpec(whole, lambda i, *_: (0, 0, 0)),
        ),
        cost_estimate=BRIEF,
        name="settle",
    )(place_of, *parts)


def canonical(member, pieces):
    pieces = list(pieces)
    bit = 1
    while bit < len(pieces):
        swap = (member & bit) != 0
        pieces = [jnp.where(swap, pieces[k ^ bit], pieces[k]) for k in range(len(pieces))]
        bit *= 2
    return pieces


def swap_perm(group, k):
    return [(z * group + m, z * group + (m ^ k)) for z in range(ZLEN) for m in range(group)]


def ring_perm(group, shift):
    return [
        (z * group + m, ((z + shift) % ZLEN) * group + m) for z in range(ZLEN) for m in range(group)
    ]


def fast_device(
    draft_ids, worker_slot, accepted, embedding, w_query, w_key, w_value, w_gate, old_state
):
    own_rows, draft = draft_ids.shape
    heads = old_state.shape[1]
    key_dim, value_dim = old_state.shape[2:]
    group = lax.axis_size("req") // ZLEN
    member = lax.axis_index("req") % group
    zpos = lax.axis_index("req") // group

    head_ids = (lax.axis_index("head") * heads + jnp.arange(heads, dtype=jnp.int32)).astype(
        jnp.float32
    )
    log_rate = jnp.log1p(-jnp.exp2(-5.0 - head_ids))

    me = member.reshape(1).astype(jnp.int32)
    where_z = zpos.reshape(1).astype(jnp.int32)
    low = lax.axis_index("head").reshape(1).astype(jnp.int32)
    target = worker_slot // own_rows
    scalars = (target, accepted, log_rate, me)

    chunks = ((0, 1), (2,), (3,))
    tokens = Asked(draft_ids, worker_slot, embedding)
    packed = pack(heads, chunks, group, me, (w_query, w_key, w_value, w_gate))

    def swaps(c):
        parts = [part if k == 0 else side(part, k) for k, part in enumerate(packed[c])]
        return jnp.concatenate(parts, axis=0)

    def up(piece):
        return lax.ppermute(piece, "req", ring_perm(group, 1))

    def down(piece):
        return lax.ppermute(piece, "req", ring_perm(group, -1))

    def side(rows, k):
        return lax.ppermute(rows, "req", swap_perm(group, k))

    def fence(*values):
        return lax.optimization_barrier(values)

    def hand_back(parts):
        return [part if k == 0 else side(part, k) for k, part in enumerate(parts)]

    plane_b, plane_a = swaps(1), swaps(0)
    one_b, three_b = up(plane_b), down(plane_b)
    heard = after(trade(tokens.table), plane_b)
    two_b = up(after(one_b, heard))
    first, finish, place_of = tokens.fetch(heard, found=(three_b, two_b))
    first, plane_a = fence(first, plane_a)
    half = finish(first)

    one_a = up(after(plane_a, half))
    three_a = down(after(plane_a, half))
    other = lax.ppermute(half, "head", [(0, 1), (1, 0)])
    half_x = side(half, 2)
    half, other, half_x = fence(half, other, half_x)
    other_x = side(other, 2)
    plane_c = swaps(2)
    other_x, one_a, plane_c = fence(other_x, one_a, plane_c)
    mine = norm(low, me, half, other, half_x, other_x)
    mine, three_a, one_a = fence(mine, three_a, one_a)
    two_a = up(one_a)
    there = side(mine, 1)

    (made_b,) = project(where_z, mine, there, (plane_b, one_b, two_b, three_b))
    mix_b, two_a, plane_c = fence(hand_back(made_b), two_a, plane_c)
    one_c, three_c = up(plane_c), down(plane_c)
    (made_a,) = project(where_z, mine, there, (plane_a, one_a, two_a, three_a))
    mix_b, one_c, made_a = fence(mix_b, one_c, made_a)
    mix_a = hand_back(made_a)
    two_c = up(one_c)
    front, new_state = retain(2, 0, 0, 1, True, True, scalars, mix_b, old_state, None, None)
    front = trade(front)
    new_state, mix_a[2], three_c, two_c = fence(new_state, mix_a[2], three_c, two_c)
    (made_c,) = project(where_z, mine, there, (plane_c, one_c, two_c, three_c))
    mix_a, made_c = fence(mix_a, made_c)
    mix_c = hand_back(made_c)
    (back,) = retain(0, 0, 0, 3, True, False, scalars, mix_a, old_state, None, None)
    (back,) = retain(1, 1, 1, 3, True, False, scalars, mix_a, old_state, back, None)
    back, mix_c = fence(back, mix_c)
    (back,) = retain(3, 0, 2, 3, True, False, scalars, mix_c, old_state, back, None)
    back, mix_a, mix_c = fence(back, mix_a, mix_c)
    back = trade(back)
    for j, at, mix in ((0, 0, mix_a), (1, 1, mix_a), (3, 0, mix_c)):
        (new_state,) = retain(j, at, 0, 1, False, True, scalars, mix, old_state, None, new_state)
    return settle(place_of, ((2,), (0, 1, 3)), [front, back]), new_state


def plain_device(
    draft_ids, worker_slot, accepted, embedding, w_query, w_key, w_value, w_gate, old_state
):
    own_rows, draft = draft_ids.shape
    tables = [
        lax.all_gather(table, "req", axis=0, tiled=True)
        for table in (w_query, w_key, w_value, w_gate)
    ]
    asked = Asked(draft_ids, worker_slot, embedding)
    half, finish, place_of = asked.fetch(trade(asked.table))
    half = finish(half)
    tokens = lax.all_gather(half, "head", axis=1, tiled=True)
    normed = layer_norm(tokens.astype(jnp.float32)).astype(jnp.bfloat16)
    raw = [jnp.dot(normed, table, preferred_element_type=jnp.float32) for table in tables]
    raw[1] = raw[1] * old_state.shape[2] ** (-0.5)
    made = [one.astype(jnp.bfloat16).reshape(own_rows, draft, -1) for one in raw]
    heads = old_state.shape[1]
    head_ids = (lax.axis_index("head") * heads + jnp.arange(heads, dtype=jnp.int32)).astype(
        jnp.float32
    )
    answer, new_state = retention(*made, old_state, accepted, head_ids)
    width = lax.axis_size("req")
    target = worker_slot // own_rows
    ahead = jnp.zeros((width,) + answer.shape[1:], answer.dtype).at[target].set(answer)
    received = lax.all_to_all(ahead, "req", split_axis=0, concat_axis=0, tiled=True)
    mine = lax.axis_index("req")
    valid = lax.all_to_all(
        (target[None, :] == jnp.arange(width)[:, None]).any(axis=1).astype(jnp.int32)[:, None],
        "req", split_axis=0, concat_axis=0, tiled=True,
    )[:, 0]
    spot = jnp.where(valid > 0, place_of, own_rows)
    hidden = jnp.zeros_like(answer).at[spot].set(received, mode="drop")
    return hidden, new_state


def solution(mesh):
    width, head_width = mesh.shape["req"], mesh.shape["head"]
    fast = head_width == 2 and width == 16
    return jax.shard_map(
        fast_device if fast else plain_device,
        mesh=mesh,
        in_specs=(
            P("req", None),
            P("req"),
            P("req"),
            P("req", "head"),
            P("req", "head"),
            P("req", "head"),
            P("req", "head"),
            P("req", "head"),
            P("req", "head", None, None),
        ),
        out_specs=(P("req", None, "head"), P("req", "head", None, None)),
        check_vma=False,
    )
```
